32 devices in a mesh: dp: 8 (over y, x, core), hid: 4 (over z).
Axes of the slice: x: 2, y: 2, z: 4, core: 2. Of those that a mesh axis runs over, the one named last changes fastest.
Arguments:
- tokens: bfloat16 [4096, 8192], P('dp', 'hid'), may hold values from -6 to 6
- up_blocks: bfloat16 [7, 64, 128, 1024], P(None, 'hid', 'dp'), may hold values from -0.1875 to 0.1875
- up_left: bfloat16 [8192, 512], P('hid'), may hold values from -0.0625 to 0.0625
- up_right: bfloat16 [512, 65536], P(None, 'hid'), may hold values from -0.25 to 0.25
- down_blocks: bfloat16 [7, 64, 1024, 128], P(None, 'hid', 'dp'), may hold values from -0.0625 to 0.0625
- down_left: bfloat16 [65536, 512], P('hid'), may hold values from -0.0234375 to 0.0234375
- down_right: bfloat16 [512, 8192], P(None, 'hid'), may hold values from -0.25 to 0.25
Outputs:
- mixed: bfloat16 [4096, 8192], P('dp', 'hid')
The draws below stay inside these ranges and needn't reach their ends.
All inputs are finite; a program needn't handle non-finite values.
Results may differ from the reference program's by a relative error of at most 0.0059.
Values may be sent and summed in bfloat16 or wider, within the bound.
A program may use at most 384 MiB of HBM per device.

```python
import jax
import jax.numpy as jnp
from jax import lax

D = 8192
FFH = 65536
BLK = 128
R = 512
NT = 7
TOK_DEV = 512
TOKENS = 4096


def steps_of(rng, extent, shards, least, largest):
    level = 1.0
    for dim, shards_of in shards:
        steps = jax.random.uniform(jax.random.fold_in(jax.random.fold_in(rng, 6), dim), (shards_of,), jnp.float32, least / len(shards), largest / len(shards))
        level = level * jnp.repeat(jnp.exp(steps), extent[dim] // shards_of).reshape((-1,) + (1,) * (len(extent) - 1 - dim))
    return level


def normal_values(stream_key, dims, spread, limit, cuts=(), held_as=jnp.bfloat16):
    values = spread * jax.random.normal(stream_key, dims, jnp.float32)
    if cuts:
        values = values * steps_of(stream_key, dims, cuts, -0.22, 0.18)
    return jnp.clip(values, -limit, limit).astype(held_as)


def setup_inputs(seed: int = 0) -> dict:
    splits = jax.random.split(jax.random.key(seed), 8)
    tokens = normal_values(splits[0], (TOKENS, D), 1.0, 6.0, ((0, 8), (1, 4)))
    up_blocks = normal_values(splits[1], (NT, D // BLK, BLK, FFH // D * BLK), (NT * BLK) ** -0.5, 0.1875, ((1, 4), (2, 8)))
    up_left = normal_values(splits[2], (D, R), D ** -0.5, 0.0625, ((0, 4),))
    up_right = normal_values(splits[3], (R, FFH), R ** -0.5, 0.25, ((1, 4),))
    down_blocks = normal_values(splits[4], (NT, D // BLK, FFH // D * BLK, BLK), (NT * (FFH // D) * BLK) ** -0.5, 0.0625, ((1, 4), (2, 8)))
    down_left = normal_values(splits[5], (FFH, R), FFH ** -0.5, 0.0234375, ((0, 4),))
    down_right = normal_values(splits[6], (R, D), R ** -0.5, 0.25, ((1, 4),))
    return {"tokens": tokens, "up_blocks": up_blocks, "up_left": up_left, "up_right": up_right, "down_blocks": down_blocks, "down_left": down_left, "down_right": down_right}


def term_offset(step_index):
    return 0 if step_index == 0 else 2 ** (step_index - 1)


def reference(tokens, up_blocks, up_left, up_right, down_blocks, down_left, down_right):
    block_count = D // BLK
    group_width = FFH // D * BLK

    def token_block(token_rows):
        row_count = token_rows.shape[0]
        pieces = token_rows.reshape(row_count, block_count, BLK).astype(jnp.float32)
        block_order = jnp.arange(block_count, dtype=jnp.int32)
        hidden_sum = jnp.zeros((row_count, block_count, group_width), jnp.float32)
        for step_index in range(NT):
            source = pieces[:, jnp.bitwise_xor(block_order, term_offset(step_index)), :]
            hidden_sum = hidden_sum + jnp.einsum("abk,bkn->abn", source, up_blocks[step_index].astype(jnp.float32))
        rank_up = jnp.dot(token_rows, up_left, preferred_element_type=jnp.float32).astype(jnp.bfloat16)
        pre_activation = hidden_sum.reshape(row_count, FFH) + jnp.dot(rank_up, up_right, preferred_element_type=jnp.float32)
        active = jax.nn.gelu(pre_activation, approximate=False).astype(jnp.bfloat16)
        grouped = active.reshape(row_count, block_count, group_width).astype(jnp.float32)
        out_sum = jnp.zeros((row_count, block_count, BLK), jnp.float32)
        for step_index in range(NT):
            contribution = jnp.einsum("abn,bnk->abk", grouped, down_blocks[step_index].astype(jnp.float32))
            out_sum = out_sum + contribution[:, jnp.bitwise_xor(block_order, term_offset(step_index)), :]
        rank_down = jnp.dot(active, down_left, preferred_element_type=jnp.float32).astype(jnp.bfloat16)
        result = out_sum.reshape(row_count, D) + jnp.dot(rank_down, down_right, preferred_element_type=jnp.float32)
        return result.astype(jnp.bfloat16)

    blocked = tokens.reshape(TOKENS // TOK_DEV, TOK_DEV, D)
    return lax.map(token_block, blocked).reshape(TOKENS, D)
```

```python
import functools

import jax
import jax.numpy as jnp
from jax import lax
from jax.experimental import pallas as pl
from jax.experimental.pallas import tpu as pltpu
from jax.sharding import PartitionSpec as P


def from_partner(block, axis, stride):
    count = lax.axis_size(axis)
    route = []
    for low in range(count):
        high = low | 1 << stride
        if high != low and high < count:
            route += [(low, high), (high, low)]
    return lax.ppermute(block, axis, route)


def swap_blocks(values, block_span, along_axis):
    full_shape = values.shape
    extent = full_shape[along_axis]
    split_shape = (
        full_shape[:along_axis]
        + (extent // (2 * block_span), 2, block_span)
        + full_shape[along_axis + 1 :]
    )
    return jnp.flip(values.reshape(split_shape), along_axis + 1).reshape(full_shape)


def shards_plain(tokens, up_blocks, up_left, up_right, down_blocks, down_left, down_right):
    token_rows = tokens.shape[0]
    local_blocks = up_blocks.shape[1]
    block_size = down_blocks.shape[3]
    term_count = up_blocks.shape[0]
    pieces = tokens.reshape(token_rows, local_blocks, block_size)
    sources = []
    for step_index in range(term_count):
        block_span = 0 if step_index == 0 else 2 ** (step_index - 1)
        if block_span == 0:
            sources.append(pieces)
        elif block_span < local_blocks:
            sources.append(swap_blocks(pieces, block_span, 1))
        else:
            swap_bit = (block_span // local_blocks).bit_length() - 1
            partner_rows = from_partner(tokens, "hid", swap_bit)
            sources.append(partner_rows.reshape(token_rows, local_blocks, block_size))
    stacked = jnp.stack(sources)
    up_full = lax.all_gather(up_blocks, "dp", axis=2, tiled=True)
    hidden_sum = jnp.einsum("tabk,tbkn->abn", stacked, up_full, preferred_element_type=jnp.float32)
    down_full = lax.all_gather(down_blocks, "dp", axis=2, tiled=True)
    rank_up = lax.psum(jnp.dot(tokens, up_left, preferred_element_type=jnp.float32), "hid").astype(
        jnp.bfloat16
    )
    pre_activation = hidden_sum.reshape(
        token_rows, hidden_sum.shape[1] * hidden_sum.shape[2]
    ) + jnp.dot(rank_up, up_right, preferred_element_type=jnp.float32)
    active = jax.nn.gelu(pre_activation, approximate=False).astype(jnp.bfloat16)
    grouped = active.reshape(token_rows, local_blocks, hidden_sum.shape[2])
    contributions = jnp.einsum(
        "abn,tbnk->tabk", grouped, down_full, preferred_element_type=jnp.float32
    )
    out_sum = jnp.zeros((token_rows, local_blocks, block_size), jnp.float32)
    for step_index in range(term_count):
        block_span = 0 if step_index == 0 else 2 ** (step_index - 1)
        if block_span == 0:
            out_sum = contributions[0]
        elif block_span < local_blocks:
            out_sum = out_sum + swap_blocks(contributions[step_index], block_span, 1)
        else:
            swap_bit = (block_span // local_blocks).bit_length() - 1
            out_sum = out_sum + from_partner(contributions[step_index], "hid", swap_bit)
    rank_down = lax.psum(
        jnp.dot(active, down_left, preferred_element_type=jnp.float32), "hid"
    ).astype(jnp.bfloat16)
    result = out_sum.reshape(token_rows, local_blocks * block_size) + jnp.dot(
        rank_down, down_right, preferred_element_type=jnp.float32
    )
    return result.astype(jnp.bfloat16)


EARLY = 6
NEAR = 5
BESIDE = 4
MESH = pl.DeviceIdType.MESH


def flip(index, bit):
    return index + bit - 2 * bit * ((index // bit) % 2)


def fused(
    tokens, up_blocks, up_left, up_right, down_blocks, down_left, down_right,
    out, up_all, down_all,
    tok, swapped, take, left, rank_up, rank_down, rank_part, rank_send, rank_in, rank_take,
    active, acc, other, w_up, w_right, w_down, w_left,
    sent, got, tok_sent, tok_got, swap_sent, swap_got, give_sent, give_got,
    far_sent, far_got, near_sent, near_got, fold_sent, fold_got,
    pair_sent, pair_got, load_sem, low_sem, pre_sem,
):
    rows = tokens.shape[0]
    terms, blocks = up_blocks.shape[0], up_blocks.shape[1]
    size = down_blocks.shape[3]
    width = up_blocks.shape[3]
    depth = terms * size
    units = blocks // 2
    span = units * size
    me, here = lax.axis_index("dp"), lax.axis_index("hid")
    half = (me // 4) % 2
    slabs = lax.axis_size("hid")
    bits = slabs.bit_length() - 1
    locals_ = terms - bits
    share = rows // 2
    sibling, across, beside = flip(me, 1), flip(me, 2), flip(me, 4)
    diagonal = flip(across, 4)
    pair_cols = 2 * size
    pairs = units // 2
    ranks = (rank_up, rank_down)

    barrier = pltpu.get_barrier_semaphore()
    for near in (sibling, across, beside):
        pl.semaphore_signal(barrier, inc=1, device_id=(near, here), device_id_type=MESH)
    for bit in range(bits):
        pl.semaphore_signal(
            barrier, inc=1, device_id=(me, flip(here, 1 << bit)), device_id_type=MESH
        )
    pl.semaphore_wait(barrier, 3 + bits)

    stages = ((up_blocks, up_all), (down_blocks, down_all))

    def remote(source, target, send, recv, device):
        return pltpu.make_async_remote_copy(
            src_ref=source, dst_ref=target, send_sem=send, recv_sem=recv,
            device_id=device, device_id_type=MESH,
        )

    def cols_of(index, count):
        return pl.ds(pl.multiple_of(index * count, count), count)

    def who_rows(who):
        return pl.ds(who * rows, rows)

    def hop(stage, kind, unit):
        blocks_ref, all_ref = stages[stage]
        if kind < 3:
            side = half if kind < 2 else 1 - half
            source, slot = blocks_ref.at[:, side * units + unit], me
            target = (sibling, across, beside)[kind]
        else:
            slot, target = ((beside, across), (across, sibling), (beside, sibling), (diagonal, sibling))[kind - 3]
        place = all_ref.at[:, unit, slot]
        if kind >= 3:
            source = place
        return remote(source, place, sent.at[stage, kind, unit], got.at[stage, kind, unit], (target, here))

    slots = [me, sibling, across, flip(across, 1), beside, flip(beside, 1), diagonal, flip(diagonal, 1)]
    stored = (w_up, w_down)

    def fetch(stage, unit, count):
        blocks_ref, all_ref = stages[stage]
        return [
            pltpu.make_async_copy(
                blocks_ref.at[:, half * units + unit] if n == 0 else all_ref.at[:, unit, slot],
                stored[stage].at[unit % 2, :, slot], load_sem.at[stage, n],
            )
            for n, slot in enumerate(slots[:count])
        ]

    def send_near(stage, unit):
        hop(stage, 1, unit).start()
        hop(stage, 0, unit).start()

    def send_beside(stage, unit):
        hop(stage, 2, unit).start()

    def forward(stage, unit):
        hop(stage, 2, unit).wait_recv()
        hop(stage, 3, unit).start()
        hop(stage, 5, unit).start()
        hop(stage, 1, unit).wait_recv()
        hop(stage, 4, unit).start()

    def relay(stage, unit):
        hop(stage, 3, unit).wait_recv()
        hop(stage, 6, unit).start()
        for kind in (0, 4, 5):
            hop(stage, kind, unit).wait_recv()
        for copy in fetch(stage, unit, 7):
            copy.start()

    def settle(stage, unit):
        copies = fetch(stage, unit, 8)
        hop(stage, 6, unit).wait_recv()
        copies[-1].start()
        for copy in copies:
            copy.wait()

    def act(action, position):
        if isinstance(position, int):
            if position < EARLY:
                action(0, position)
            elif position == EARLY:
                action(1, 0)
            elif position <= units:
                action(0, position - 1)
            elif position < 2 * units:
                action(1, position - units)
            return
        pl.when(position < EARLY)(lambda: action(0, position))
        pl.when(position == EARLY)(lambda: action(1, 0))
        pl.when((position > EARLY) & (position <= units))(lambda: action(0, position - 1))
        pl.when((position > units) & (position < 2 * units))(lambda: action(1, position - units))

    def feed(position):
        act(send_near, position + NEAR)
        act(send_beside, position + BESIDE)

    def pump(position):
        act(forward, position + 2)
        act(relay, position + 1)

    def lend(part, pair):
        side = 1 - half if part == 0 else half
        return remote(
            tokens.at[:, cols_of(side * pairs + pair, pair_cols)],
            tok.at[who_rows(1), pl.ds(pl.multiple_of(part * span + pair * pair_cols, pair_cols), pair_cols)],
            tok_sent.at[part, pair], tok_got.at[part, pair], (beside, here),
        )

    def swap(bit, who, pair):
        cols = cols_of(pair, pair_cols)
        if who == 0:
            source = tokens.at[:, cols_of(half * pairs + pair, pair_cols)]
        else:
            source = tok.at[who_rows(1), cols]
        return remote(
            source, swapped.at[bit, who_rows(who), cols],
            swap_sent.at[bit, who, pair], swap_got.at[bit, who, pair], (me, flip(here, 1 << bit)),
        )

    def swaps(who, pair):
        for bit in reversed(range(bits)):
            swap(bit, who, pair).start()

    def hand(bit, who, unit):
        cols = cols_of(unit, size)
        return remote(
            swapped.at[bit, who_rows(who), cols], take.at[bit, who_rows(who), cols],
            give_sent.at[bit, who, unit], give_got.at[bit, who, unit], (me, flip(here, 1 << bit)),
        )

    quarter = left.shape[0] // 2
    per = units // quarter

    def back(side, unit):
        sends, gets = ((near_sent, near_got), (far_sent, far_got))[side]
        source = pl.ds(pl.multiple_of(side * span + unit * size, size), size)
        return remote(
            tok.at[who_rows(1), source],
            left.at[(1 - side) * quarter + unit // per, :, cols_of(unit % per, size)],
            sends.at[unit], gets.at[unit], (beside, here),
        )

    halves = [
        pl.ds(pl.multiple_of((here % 2) * share, share), share),
        pl.ds(pl.multiple_of((1 - here % 2) * share, share), share),
    ]

    def fold(which, step):
        if step == 0:
            source, target = rank_send.at[which, halves[1]], rank_in.at[which, 0]
        elif step == 1:
            source, target = rank_send.at[which, halves[0]], rank_in.at[which, 1]
        else:
            source = target = ranks[which].at[halves[0]]
        return remote(
            source, target, fold_sent.at[which, step], fold_got.at[which, step],
            (me, flip(here, 2 if step == 1 else 1)),
        )

    def fold_first(which):
        rank_send[which, :, :] = rank_part[:rows, :].astype(jnp.bfloat16)
        fold(which, 0).start()

    def fold_second(which):
        fold(which, 0).wait_recv()
        total = rank_part[halves[0], :] + rank_in[which, 0].astype(jnp.float32)
        rank_part[halves[0], :] = total
        rank_send[which, halves[0], :] = total.astype(jnp.bfloat16)
        fold(which, 1).start()

    def fold_third(which):
        fold(which, 1).wait_recv()
        total = rank_part[halves[0], :] + rank_in[which, 1].astype(jnp.float32)
        ranks[which][halves[0], :] = total.astype(jnp.bfloat16)
        fold(which, 2).start()

    def pair_rank(which):
        if which == 0:
            source, target = rank_up.at[who_rows(0)], rank_up.at[who_rows(1)]
        else:
            source, target = rank_up.at[who_rows(1)], rank_take
        return remote(source, target, pair_sent.at[which], pair_got.at[which], (beside, here))

    chunk = span // quarter

    pre = [
        pltpu.make_async_copy(
            tokens.at[:, cols_of(half * (1 - n) + (1 - half) * n, span)],
            tok.at[who_rows(0), pl.ds(n * span, span)], pre_sem.at[n],
        )
        for n in range(2)
    ]
    for n in range(2):
        for q in range(quarter):
            at = (half * (1 - n) + (1 - half) * n) * quarter + q
            pre.append(pltpu.make_async_copy(
                up_left.at[cols_of(at, chunk)], left.at[n * quarter + q], pre_sem.at[2 + n * quarter + q]
            ))
    final = [
        pltpu.make_async_copy(
            down_right.at[:, cols_of(half * (1 - n) + (1 - half) * n, span)],
            tok.at[who_rows(0), pl.ds(n * span, span)], pre_sem.at[n],
        )
        for n in range(2)
    ]

    def low(unit, slot):
        at = half * units + unit
        return (
            pltpu.make_async_copy(up_right.at[:, cols_of(at, width)], w_right.at[slot], low_sem.at[0, slot]),
            pltpu.make_async_copy(down_left.at[cols_of(at, width)], w_left.at[slot], low_sem.at[1, slot]),
        )

    for copy in pre:
        copy.start()
    lend(0, 0).start()
    lend(0, 1).start()
    act(send_beside, 0)
    act(send_near, 0)
    swap(1, 0, 0).start()
    lend(0, 2).start()
    act(send_beside, 1)
    lend(1, 0).start()
    for position in range(1, NEAR - 1):
        act(send_near, position)
    for copy in low(0, 0):
        copy.start()
    for copy in pre:
        copy.wait()
    total = jnp.dot(tok[:rows, :chunk], left[0], preferred_element_type=jnp.float32)
    for n in range(1, 2 * quarter):
        total += jnp.dot(
            tok[:rows, n * chunk : (n + 1) * chunk], left[n], preferred_element_type=jnp.float32
        )
    rank_part[:rows, :] = total
    fold_first(0)
    swap(0, 0, 0).start()
    acc[...] = jnp.zeros_like(acc)
    fold_second(0)
    swap(1, 0, 1).start()
    lend(0, 0).wait_recv()
    act(forward, 0)
    fold_third(0)
    swaps(1, 0)
    swap(0, 0, 1).start()
    rank_part[...] = jnp.zeros_like(rank_part)
    act(forward, 1)
    act(send_near, NEAR - 1)
    fold(0, 2).wait_recv()
    pair_rank(0).start()
    act(send_beside, 2)
    lend(0, 3).start()
    for position in range(3, BESIDE):
        act(send_beside, position)
    lend(1, 1).start()
    lend(0, 1).wait_recv()
    swaps(1, 1)
    act(relay, 0)
    lend(0, 2).wait_recv()
    swaps(0, 2)
    swaps(1, 2)
    swaps(0, 3)
    pair_rank(0).wait_recv()

    tile = 256

    def up_begin(unit):
        settle(0, unit)

    def up_work(unit, position):
        slot = unit % 2
        for copy in low(unit, slot):
            copy.wait()
        parts = []
        for term in range(terms):
            if term < locals_ - 1:
                at = unit if term == 0 else flip(unit, 1 << (term - 1))
                parts.append(tok[:, cols_of(at, size)])
            elif term == locals_ - 1:
                parts.append(tok[:, pl.ds(pl.multiple_of(span + unit * size, size), size)])
            else:
                parts.append(swapped[term - locals_, :, cols_of(unit, size)])
        source = jnp.concatenate(parts, axis=1)
        coords = rank_up[...]
        for n in range(width // tile):
            cut = slice(n * tile, (n + 1) * tile)
            weights = w_up[slot, :, :, :, cut].reshape(depth, tile)
            pre_act = jnp.dot(source, weights, preferred_element_type=jnp.float32)
            pre_act += jnp.dot(coords, w_right[slot, :, cut], preferred_element_type=jnp.float32)
            value = 0.5 * pre_act * (1.0 + lax.erf(pre_act * (0.5 ** 0.5)))
            start = pl.multiple_of(unit * width + n * tile, tile)
            active[:, pl.ds(start, tile)] = value.astype(jnp.bfloat16)
            if n == width // tile - 2:
                pump(position)
        rank_part[...] += jnp.dot(
            active[:, cols_of(unit, width)], w_left[slot], preferred_element_type=jnp.float32
        )

    def arrive(pair):
        for bit in range(bits):
            for who in range(2):
                swap(bit, who, pair).wait_recv()
        lend(1, pair).wait_recv()

    def up_unit(unit, carry):
        pair = unit // 2
        pl.when((unit % 2 == 1) & (pair + 2 < pairs))(lambda: lend(1, pair + 2).start())
        feed(unit)
        up_begin(unit)

        @pl.when(unit == 2)
        def _():
            lend(0, pairs - 1).wait_recv()
            swaps(1, pairs - 1)

        for copy in low(unit + 1, (unit + 1) % 2):
            copy.start()
        pl.when(unit % 2 == 0)(functools.partial(arrive, pair))
        up_work(unit, unit)
        return carry

    def close(unit):
        mine, cols = who_rows(1), cols_of(unit, size)
        total = acc[mine, cols]
        for bit in range(bits):
            hand(bit, 1, unit).wait_recv()
            total = total + take[bit, mine, cols].astype(jnp.float32)
        tok[mine, cols] = total.astype(jnp.bfloat16)
        back(0, unit).start()

    def down_work(unit, middle=lambda: None):
        slot = unit % 2
        source = active[:, cols_of(unit, width)]
        order = [*range(locals_, terms), locals_ - 1, *range(locals_ - 1)]
        for first in range(0, terms, 2):
            pair = order[first : first + 2]
            if first == 4:
                middle()
                pump(EARLY if isinstance(unit, int) else unit + units)
            weights = jnp.concatenate([w_down[slot, term].reshape(width, size) for term in pair], axis=1)
            product = jnp.dot(source, weights, preferred_element_type=jnp.float32)
            for n, term in enumerate(pair):
                piece = product[:, n * size : (n + 1) * size]
                if term < locals_ - 1:
                    at = unit if term == 0 else flip(unit, 1 << (term - 1))
                    acc[:, cols_of(at, size)] += piece
                elif term == locals_ - 1:
                    other[:, cols_of(unit, size)] = piece[:rows]
                    far = pl.ds(pl.multiple_of(span + unit * size, size), size)
                    tok[who_rows(1), far] = piece[rows:].astype(jnp.bfloat16)
                    back(1, unit).start()
                else:
                    bit = term - locals_
                    swapped[bit, :, cols_of(unit, size)] = piece.astype(jnp.bfloat16)
                    if term == terms - 1:
                        for who in (1, 0):
                            for bit in reversed(range(bits)):
                                hand(bit, who, unit).start()

    def down_begin(unit):
        settle(1, unit)

    def down_unit(unit, carry):
        feed(unit + units)
        down_begin(unit)

        def middle():
            @pl.when(unit == 2)
            def _():
                pair_rank(1).wait_recv()
                rank_part[:rows, :] += rank_take[...].astype(jnp.float32)
                fold_first(1)

            pl.when(unit == 4)(lambda: fold_second(1))
            pl.when(unit == 6)(lambda: fold_third(1))

        down_work(unit, middle)
        pl.when(unit >= units // 2)(lambda: close(unit - units // 2))
        return carry

    lax.fori_loop(0, EARLY, up_unit, 0)
    feed(EARLY)
    down_begin(0)
    down_work(0)
    for unit in range(EARLY, units):
        feed(unit + 1)
        up_begin(unit)
        if unit + 1 < units:
            for copy in low(unit + 1, (unit + 1) % 2):
                copy.start()
        if unit % 2 == 0:
            arrive(unit // 2)
        up_work(unit, unit + 1)
    for copy in final:
        copy.start()
    rank_up[rows:, :] = rank_part[rows:, :].astype(jnp.bfloat16)
    pair_rank(1).start()
    for pair in range(pairs):
        for bit in range(bits):
            swap(bit, 1, pair).wait_send()
    lax.fori_loop(1, units, down_unit, 0)
    fold(1, 2).wait_recv()
    for copy in final:
        copy.wait()
    step = 512
    for n in range(span // step):
        cut = slice(n * step, (n + 1) * step)
        acc[:rows, cut] += jnp.dot(rank_down[...], tok[:rows, cut], preferred_element_type=jnp.float32)
    lax.fori_loop(units // 2, units, lambda unit, carry: (close(unit), carry)[1], 0)

    def finish(unit, carry):
        mine, cols = who_rows(0), cols_of(unit, size)
        far = pl.ds(pl.multiple_of(span + unit * size, size), size)
        back(1, unit).wait_recv()
        total = acc[mine, cols] + left[unit // per, :, cols_of(unit % per, size)].astype(jnp.float32)
        for bit in range(bits):
            hand(bit, 0, unit).wait_recv()
            total = total + take[bit, mine, cols].astype(jnp.float32)
        out[:, cols_of(half * units + unit, size)] = total.astype(jnp.bfloat16)
        total = other[:, cols] + jnp.dot(rank_down[...], tok[mine, far], preferred_element_type=jnp.float32)
        back(0, unit).wait_recv()
        total = total + left[quarter + unit // per, :, cols_of(unit % per, size)].astype(jnp.float32)
        out[:, cols_of((1 - half) * units + unit, size)] = total.astype(jnp.bfloat16)
        for stage in range(2):
            for kind in range(7):
                hop(stage, kind, unit).wait_send()
        for bit in range(bits):
            for who in range(2):
                hand(bit, who, unit).wait_send()
        for side in range(2):
            back(side, unit).wait_send()
        return carry

    lax.fori_loop(0, units, finish, 0)
    for pair in range(pairs):
        for part in range(2):
            lend(part, pair).wait_send()
        for bit in range(bits):
            swap(bit, 0, pair).wait_send()
    for which in range(2):
        pair_rank(which).wait_send()
        for step in range(3):
            fold(which, step).wait_send()


def shards_fused(tokens, up_blocks, up_left, up_right, down_blocks, down_left, down_right):
    rows, features = tokens.shape
    terms, blocks, up_rows, width = up_blocks.shape
    down_rows, size = down_blocks.shape[2:]
    rank = up_left.shape[1]
    count, slabs = lax.axis_size("dp"), lax.axis_size("hid")
    bits = slabs.bit_length() - 1
    units, span = blocks // 2, features // 2
    pairs = units // 2
    any_ = pl.BlockSpec(memory_space=pl.ANY)
    bf, f32 = jnp.bfloat16, jnp.float32
    dma = pltpu.SemaphoreType.DMA
    out, _, _ = pl.pallas_call(
        fused,
        out_shape=(
            jax.ShapeDtypeStruct((rows, features), bf),
            jax.ShapeDtypeStruct((terms, units, count, up_rows, width), bf),
            jax.ShapeDtypeStruct((terms, units, count, down_rows, size), bf),
        ),
        in_specs=[any_] * 7,
        out_specs=(pl.BlockSpec(memory_space=pltpu.VMEM), any_, any_),
        scratch_shapes=[
            pltpu.VMEM((2 * rows, features), bf),
            pltpu.VMEM((bits, 2 * rows, span), bf),
            pltpu.VMEM((bits, 2 * rows, span), bf),
            pltpu.VMEM((features // rows, rows, rank), bf),
            pltpu.VMEM((2 * rows, rank), bf),
            pltpu.VMEM((rows, rank), bf),
            pltpu.VMEM((2 * rows, rank), f32),
            pltpu.VMEM((2, rows, rank), bf),
            pltpu.VMEM((2, 2, rows // 2, rank), bf),
            pltpu.VMEM((rows, rank), bf),
            pltpu.VMEM((2 * rows, units * width), bf),
            pltpu.VMEM((2 * rows, span), f32),
            pltpu.VMEM((rows, span), f32),
            pltpu.VMEM((2, terms, count, up_rows, width), bf),
            pltpu.VMEM((2, rank, width), bf),
            pltpu.VMEM((2, terms, count, down_rows, size), bf),
            pltpu.VMEM((2, width, rank), bf),
            dma((2, 7, units)), dma((2, 7, units)),
            dma((2, pairs)), dma((2, pairs)),
            dma((bits, 2, pairs)), dma((bits, 2, pairs)),
            dma((bits, 2, units)), dma((bits, 2, units)),
            dma((units,)), dma((units,)), dma((units,)), dma((units,)),
            dma((2, 3)), dma((2, 3)),
            dma((2,)), dma((2,)),
            dma((2, count)), dma((2, 2)), dma((2 + features // rows,)),
        ],
        compiler_params=pltpu.CompilerParams(
            collective_id=0, has_side_effects=True, vmem_limit_bytes=62 * 1024 * 1024
        ),
    )(tokens, up_blocks, up_left, up_right, down_blocks, down_left, down_right)
    return out


def shards(tokens, up_blocks, up_left, *rest):
    terms, blocks, up_rows, _ = up_blocks.shape
    rows, features = tokens.shape
    slabs = lax.axis_size("hid")
    reach = blocks.bit_length() - 1 + slabs.bit_length()
    fits = (
        lax.axis_size("dp") == 8
        and up_rows % 16 == 0
        and blocks == 16
        and terms == reach
        and slabs == 4
        and rows == 512
        and features == 4 * rows
        and up_left.shape[1] == rows
    )
    body = shards_fused if fits else shards_plain
    return body(tokens, up_blocks, up_left, *rest)


def solution(mesh):
    placed = (
        P("dp", "hid"),
        P(None, "hid", "dp", None),
        P("hid", None),
        P(None, "hid"),
        P(None, "hid", "dp", None),
        P("hid", None),
        P(None, "hid"),
    )
    return jax.shard_map(
        shards, mesh=mesh, in_specs=placed, out_specs=P("dp", "hid"), check_vma=False
    )
```

```python
import functools

import jax
import jax.numpy as jnp
from jax import lax
from jax.experimental import pallas as pl
from jax.experimental.pallas import tpu as pltpu
from jax.sharding import PartitionSpec as P


def from_partner(block, axis, stride):
    count = lax.axis_size(axis)
    route = []
    for low in range(count):
        high = low | 1 << stride
        if high != low and high < count:
            route += [(low, high), (high, low)]
    return lax.ppermute(block, axis, route)


def swap_blocks(values, block_span, along_axis):
    full_shape = values.shape
    extent = full_shape[along_axis]
    split_shape = (
        full_shape[:along_axis]
        + (extent // (2 * block_span), 2, block_span)
        + full_shape[along_axis + 1 :]
    )
    return jnp.flip(values.reshape(split_shape), along_axis + 1).reshape(full_shape)


def shards_plain(tokens, up_blocks, up_left, up_right, down_blocks, down_left, down_right):
    token_rows = tokens.shape[0]
    local_blocks = up_blocks.shape[1]
    block_size = down_blocks.shape[3]
    term_count = up_blocks.shape[0]
    pieces = tokens.reshape(token_rows, local_blocks, block_size)
    sources = []
    for step_index in range(term_count):
        block_span = 0 if step_index == 0 else 2 ** (step_index - 1)
        if block_span == 0:
            sources.append(pieces)
        elif block_span < local_blocks:
            sources.append(swap_blocks(pieces, block_span, 1))
        else:
            swap_bit = (block_span // local_blocks).bit_length() - 1
            partner_rows = from_partner(tokens, "hid", swap_bit)
            sources.append(partner_rows.reshape(token_rows, local_blocks, block_size))
    stacked = jnp.stack(sources)
    up_full = lax.all_gather(up_blocks, "dp", axis=2, tiled=True)
    hidden_sum = jnp.einsum("tabk,tbkn->abn", stacked, up_full, preferred_element_type=jnp.float32)
    down_full = lax.all_gather(down_blocks, "dp", axis=2, tiled=True)
    rank_up = lax.psum(jnp.dot(tokens, up_left, preferred_element_type=jnp.float32), "hid").astype(
        jnp.bfloat16
    )
    pre_activation = hidden_sum.reshape(
        token_rows, hidden_sum.shape[1] * hidden_sum.shape[2]
    ) + jnp.dot(rank_up, up_right, preferred_element_type=jnp.float32)
    active = jax.nn.gelu(pre_activation, approximate=False).astype(jnp.bfloat16)
    grouped = active.reshape(token_rows, local_blocks, hidden_sum.shape[2])
    contributions = jnp.einsum(
        "abn,tbnk->tabk", grouped, down_full, preferred_element_type=jnp.float32
    )
    out_sum = jnp.zeros((token_rows, local_blocks, block_size), jnp.float32)
    for step_index in range(term_count):
        block_span = 0 if step_index == 0 else 2 ** (step_index - 1)
        if block_span == 0:
            out_sum = contributions[0]
        elif block_span < local_blocks:
            out_sum = out_sum + swap_blocks(contributions[step_index], block_span, 1)
        else:
            swap_bit = (block_span // local_blocks).bit_length() - 1
            out_sum = out_sum + from_partner(contributions[step_index], "hid", swap_bit)
    rank_down = lax.psum(
        jnp.dot(active, down_left, preferred_element_type=jnp.float32), "hid"
    ).astype(jnp.bfloat16)
    result = out_sum.reshape(token_rows, local_blocks * block_size) + jnp.dot(
        rank_down, down_right, preferred_element_type=jnp.float32
    )
    return result.astype(jnp.bfloat16)


EARLY = 5
NEAR = 5
BESIDE = 4
FOLDS = (4, 5, 6)
MESH = pl.DeviceIdType.MESH


def flip(index, bit):
    return index + bit - 2 * bit * ((index // bit) % 2)


def fused(
    tokens, up_blocks, up_left, up_right, down_blocks, down_left, down_right,
    out, up_all, down_all,
    tok, swapped, take, left, rank_up, rank_down, rank_part, rank_send, rank_in, rank_take,
    active, acc, other, w_up, w_right, w_down, w_left,
    sent, got, tok_sent, tok_got, swap_sent, swap_got, give_sent, give_got,
    far_sent, far_got, near_sent, near_got, fold_sent, fold_got,
    pair_sent, pair_got, load_sem, low_sem, pre_sem,
):
    rows = tokens.shape[0]
    terms, blocks = up_blocks.shape[0], up_blocks.shape[1]
    size = down_blocks.shape[3]
    width = up_blocks.shape[3]
    depth = terms * size
    units = blocks // 2
    span = units * size
    me, here = lax.axis_index("dp"), lax.axis_index("hid")
    half = (me // 4) % 2
    slabs = lax.axis_size("hid")
    bits = slabs.bit_length() - 1
    locals_ = terms - bits
    share = rows // 2
    sibling, across, beside = flip(me, 1), flip(me, 2), flip(me, 4)
    diagonal = flip(across, 4)
    pair_cols = 2 * size
    pairs = units // 2
    ranks = (rank_up, rank_down)

    barrier = pltpu.get_barrier_semaphore()
    for near in (sibling, across, beside):
        pl.semaphore_signal(barrier, inc=1, device_id=(near, here), device_id_type=MESH)
    for bit in range(bits):
        pl.semaphore_signal(
            barrier, inc=1, device_id=(me, flip(here, 1 << bit)), device_id_type=MESH
        )
    pl.semaphore_wait(barrier, 3 + bits)

    stages = ((up_blocks, up_all), (down_blocks, down_all))

    def remote(source, target, send, recv, device):
        return pltpu.make_async_remote_copy(
            src_ref=source, dst_ref=target, send_sem=send, recv_sem=recv,
            device_id=device, device_id_type=MESH,
        )

    def cols_of(index, count):
        return pl.ds(pl.multiple_of(index * count, count), count)

    def who_rows(who):
        return pl.ds(who * rows, rows)

    def hop(stage, kind, unit):
        blocks_ref, all_ref = stages[stage]
        if kind < 3:
            side = half if kind < 2 else 1 - half
            source, slot = blocks_ref.at[:, side * units + unit], me
            target = (sibling, across, beside)[kind]
        else:
            slot, target = ((beside, across), (across, sibling), (beside, sibling), (diagonal, sibling))[kind - 3]
        place = all_ref.at[:, unit, slot]
        if kind >= 3:
            source = place
        return remote(source, place, sent.at[stage, kind, unit], got.at[stage, kind, unit], (target, here))

    slots = [me, sibling, across, flip(across, 1), beside, flip(beside, 1), diagonal, flip(diagonal, 1)]
    stored = (w_up, w_down)

    def fetch(stage, unit, count):
        blocks_ref, all_ref = stages[stage]
        return [
            pltpu.make_async_copy(
                blocks_ref.at[:, half * units + unit] if n == 0 else all_ref.at[:, unit, slot],
                stored[stage].at[unit % 2, :, slot], load_sem.at[stage, n],
            )
            for n, slot in enumerate(slots[:count])
        ]

    def send_near(stage, unit):
        hop(stage, 1, unit).start()
        hop(stage, 0, unit).start()

    def send_beside(stage, unit):
        hop(stage, 2, unit).start()

    def forward(stage, unit):
        hop(stage, 2, unit).wait_recv()
        hop(stage, 3, unit).start()
        hop(stage, 5, unit).start()
        hop(stage, 1, unit).wait_recv()
        hop(stage, 4, unit).start()

    def relay(stage, unit):
        hop(stage, 3, unit).wait_recv()
        hop(stage, 6, unit).start()
        for kind in (0, 4, 5):
            hop(stage, kind, unit).wait_recv()
        for copy in fetch(stage, unit, 7):
            copy.start()

    def settle(stage, unit):
        copies = fetch(stage, unit, 8)
        hop(stage, 6, unit).wait_recv()
        copies[-1].start()
        for copy in copies:
            copy.wait()

    late = 2 * units - EARLY

    def act(action, position):
        if isinstance(position, int):
            if position < EARLY:
                action(0, position)
            elif position < late:
                turn = position - EARLY
                action(1 - turn % 2, turn // 2 + EARLY * (turn % 2))
            elif position < 2 * units:
                action(1, position - units)
            return
        turn = position - EARLY
        pl.when(position < EARLY)(lambda: action(0, position))
        between = (position >= EARLY) & (position < late)
        pl.when(between & (turn % 2 == 0))(lambda: action(1, turn // 2))
        pl.when(between & (turn % 2 == 1))(lambda: action(0, turn // 2 + EARLY))
        pl.when((position >= late) & (position < 2 * units))(lambda: action(1, position - units))

    def feed(position):
        act(send_near, position + NEAR)
        act(send_beside, position + BESIDE)

    def pump(position):
        act(forward, position + 2)
        act(relay, position + 1)

    def lend(part, pair):
        side = 1 - half if part == 0 else half
        return remote(
            tokens.at[:, cols_of(side * pairs + pair, pair_cols)],
            tok.at[who_rows(1), pl.ds(pl.multiple_of(part * span + pair * pair_cols, pair_cols), pair_cols)],
            tok_sent.at[part, pair], tok_got.at[part, pair], (beside, here),
        )

    def swap(bit, who, pair):
        cols = cols_of(pair, pair_cols)
        if who == 0:
            source = tokens.at[:, cols_of(half * pairs + pair, pair_cols)]
        else:
            source = tok.at[who_rows(1), cols]
        return remote(
            source, swapped.at[bit, who_rows(who), cols],
            swap_sent.at[bit, who, pair], swap_got.at[bit, who, pair], (me, flip(here, 1 << bit)),
        )

    def swaps(who, pair):
        for bit in reversed(range(bits)):
            swap(bit, who, pair).start()

    def hand(bit, who, unit):
        cols = cols_of(unit, size)
        return remote(
            swapped.at[bit, who_rows(who), cols], take.at[bit, who_rows(who), cols],
            give_sent.at[bit, who, unit], give_got.at[bit, who, unit], (me, flip(here, 1 << bit)),
        )

    quarter = left.shape[0] // 2
    per = units // quarter

    def back(side, unit):
        sends, gets = ((near_sent, near_got), (far_sent, far_got))[side]
        source = pl.ds(pl.multiple_of(side * span + unit * size, size), size)
        return remote(
            tok.at[who_rows(1), source],
            left.at[(1 - side) * quarter + unit // per, :, cols_of(unit % per, size)],
            sends.at[unit], gets.at[unit], (beside, here),
        )

    halves = [
        pl.ds(pl.multiple_of((here % 2) * share, share), share),
        pl.ds(pl.multiple_of((1 - here % 2) * share, share), share),
    ]

    def fold(which, step):
        if step == 0:
            source, target = rank_send.at[which, halves[1]], rank_in.at[which, 0]
        elif step == 1:
            source, target = rank_send.at[which, halves[0]], rank_in.at[which, 1]
        else:
            source = target = ranks[which].at[halves[0]]
        return remote(
            source, target, fold_sent.at[which, step], fold_got.at[which, step],
            (me, flip(here, 2 if step == 1 else 1)),
        )

    def fold_first(which):
        rank_send[which, :, :] = rank_part[:rows, :].astype(jnp.bfloat16)
        fold(which, 0).start()

    def fold_second(which):
        fold(which, 0).wait_recv()
        total = rank_part[halves[0], :] + rank_in[which, 0].astype(jnp.float32)
        rank_part[halves[0], :] = total
        rank_send[which, halves[0], :] = total.astype(jnp.bfloat16)
        fold(which, 1).start()

    def fold_third(which):
        fold(which, 1).wait_recv()
        total = rank_part[halves[0], :] + rank_in[which, 1].astype(jnp.float32)
        ranks[which][halves[0], :] = total.astype(jnp.bfloat16)
        fold(which, 2).start()

    def pair_rank(which):
        if which == 0:
            source, target = rank_up.at[who_rows(0)], rank_up.at[who_rows(1)]
        else:
            source, target = rank_up.at[who_rows(1)], rank_take
        return remote(source, target, pair_sent.at[which], pair_got.at[which], (beside, here))

    chunk = span // quarter

    pre = [
        pltpu.make_async_copy(
            tokens.at[:, cols_of(half * (1 - n) + (1 - half) * n, span)],
            tok.at[who_rows(0), pl.ds(n * span, span)], pre_sem.at[n],
        )
        for n in range(2)
    ]
    for n in range(2):
        for q in range(quarter):
            at = (half * (1 - n) + (1 - half) * n) * quarter + q
            pre.append(pltpu.make_async_copy(
                up_left.at[cols_of(at, chunk)], left.at[n * quarter + q], pre_sem.at[2 + n * quarter + q]
            ))
    final = [
        pltpu.make_async_copy(
            down_right.at[:, cols_of(half * (1 - n) + (1 - half) * n, span)],
            tok.at[who_rows(0), pl.ds(n * span, span)], pre_sem.at[n],
        )
        for n in range(2)
    ]

    def low(unit, slot):
        at = half * units + unit
        return (
            pltpu.make_async_copy(up_right.at[:, cols_of(at, width)], w_right.at[slot], low_sem.at[0, slot]),
            pltpu.make_async_copy(down_left.at[cols_of(at, width)], w_left.at[slot], low_sem.at[1, slot]),
        )

    for copy in pre:
        copy.start()
    lend(0, 0).start()
    lend(0, 1).start()
    act(send_beside, 0)
    act(send_near, 0)
    swap(1, 0, 0).start()
    lend(0, 2).start()
    act(send_beside, 1)
    lend(1, 0).start()
    for position in range(1, NEAR - 1):
        act(send_near, position)
    for copy in low(0, 0):
        copy.start()
    for copy in pre:
        copy.wait()
    total = jnp.dot(tok[:rows, :chunk], left[0], preferred_element_type=jnp.float32)
    for n in range(1, 2 * quarter):
        total += jnp.dot(
            tok[:rows, n * chunk : (n + 1) * chunk], left[n], preferred_element_type=jnp.float32
        )
    rank_part[:rows, :] = total
    fold_first(0)
    swap(0, 0, 0).start()
    acc[...] = jnp.zeros_like(acc)
    fold_second(0)
    swap(1, 0, 1).start()
    lend(0, 0).wait_recv()
    act(forward, 0)
    fold_third(0)
    swaps(1, 0)
    swap(0, 0, 1).start()
    rank_part[...] = jnp.zeros_like(rank_part)
    act(forward, 1)
    act(send_near, NEAR - 1)
    fold(0, 2).wait_recv()
    pair_rank(0).start()
    act(send_beside, 2)
    lend(0, 3).start()
    for position in range(3, BESIDE):
        act(send_beside, position)
    lend(1, 1).start()
    lend(0, 1).wait_recv()
    swaps(1, 1)
    act(relay, 0)
    lend(0, 2).wait_recv()
    swaps(0, 2)
    swaps(1, 2)
    swaps(0, 3)
    pair_rank(0).wait_recv()

    tile = 256

    def up_begin(unit):
        settle(0, unit)

    def up_work(unit, position):
        slot = unit % 2
        for copy in low(unit, slot):
            copy.wait()
        parts = []
        for term in range(terms):
            if term < locals_ - 1:
                at = unit if term == 0 else flip(unit, 1 << (term - 1))
                parts.append(tok[:, cols_of(at, size)])
            elif term == locals_ - 1:
                parts.append(tok[:, pl.ds(pl.multiple_of(span + unit * size, size), size)])
            else:
                parts.append(swapped[term - locals_, :, cols_of(unit, size)])
        source = jnp.concatenate(parts, axis=1)
        coords = rank_up[...]
        for n in range(width // tile):
            cut = slice(n * tile, (n + 1) * tile)
            weights = w_up[slot, :, :, :, cut].reshape(depth, tile)
            pre_act = jnp.dot(source, weights, preferred_element_type=jnp.float32)
            pre_act += jnp.dot(coords, w_right[slot, :, cut], preferred_element_type=jnp.float32)
            value = 0.5 * pre_act * (1.0 + lax.erf(pre_act * (0.5 ** 0.5)))
            start = pl.multiple_of(unit * width + n * tile, tile)
            active[:, pl.ds(start, tile)] = value.astype(jnp.bfloat16)
            if n == width // tile - 2:
                pump(position)
        rank_part[...] += jnp.dot(
            active[:, cols_of(unit, width)], w_left[slot], preferred_element_type=jnp.float32
        )

    def arrive(pair):
        for bit in range(bits):
            for who in range(2):
                swap(bit, who, pair).wait_recv()
        lend(1, pair).wait_recv()

    def up_unit(unit, carry):
        pair = unit // 2
        pl.when((unit % 2 == 1) & (pair + 2 < pairs))(lambda: lend(1, pair + 2).start())
        feed(unit)
        up_begin(unit)

        @pl.when(unit == 2)
        def _():
            lend(0, pairs - 1).wait_recv()
            swaps(1, pairs - 1)

        for copy in low(unit + 1, (unit + 1) % 2):
            copy.start()
        pl.when(unit % 2 == 0)(functools.partial(arrive, pair))
        up_work(unit, unit)
        return carry

    def close(unit):
        mine, cols = who_rows(1), cols_of(unit, size)
        total = acc[mine, cols]
        for bit in range(bits):
            hand(bit, 1, unit).wait_recv()
            total = total + take[bit, mine, cols].astype(jnp.float32)
        tok[mine, cols] = total.astype(jnp.bfloat16)
        back(0, unit).start()

    def down_work(unit, position, middle=lambda: None):
        slot = unit % 2
        source = active[:, cols_of(unit, width)]
        order = [*range(locals_, terms), locals_ - 1, *range(locals_ - 1)]
        for first in range(0, terms, 2):
            pair = order[first : first + 2]
            if first == 4:
                middle()
                pump(position)
            weights = jnp.concatenate([w_down[slot, term].reshape(width, size) for term in pair], axis=1)
            product = jnp.dot(source, weights, preferred_element_type=jnp.float32)
            for n, term in enumerate(pair):
                piece = product[:, n * size : (n + 1) * size]
                if term < locals_ - 1:
                    at = unit if term == 0 else flip(unit, 1 << (term - 1))
                    acc[:, cols_of(at, size)] += piece
                elif term == locals_ - 1:
                    other[:, cols_of(unit, size)] = piece[:rows]
                    far = pl.ds(pl.multiple_of(span + unit * size, size), size)
                    tok[who_rows(1), far] = piece[rows:].astype(jnp.bfloat16)
                    back(1, unit).start()
                else:
                    bit = term - locals_
                    swapped[bit, :, cols_of(unit, size)] = piece.astype(jnp.bfloat16)
                    if term == terms - 1:
                        for who in (1, 0):
                            for bit in reversed(range(bits)):
                                hand(bit, who, unit).start()

    def down_begin(unit):
        settle(1, unit)

    def down_unit(unit, carry):
        feed(unit + units)
        down_begin(unit)

        def middle():
            @pl.when(unit == FOLDS[0])
            def _():
                pair_rank(1).wait_recv()
                rank_part[:rows, :] += rank_take[...].astype(jnp.float32)
                fold_first(1)

            pl.when(unit == FOLDS[1])(lambda: fold_second(1))
            pl.when(unit == FOLDS[2])(lambda: fold_third(1))

        down_work(unit, unit + units, middle)
        pl.when(unit >= units // 2)(lambda: close(unit - units // 2))
        return carry

    lax.fori_loop(0, EARLY, up_unit, 0)

    def both(turn, carry):
        position = EARLY + 2 * turn
        feed(position)
        down_begin(turn)
        down_work(turn, position)
        unit = EARLY + turn
        feed(position + 1)
        up_begin(unit)

        @pl.when(unit + 1 < units)
        def _():
            for copy in low(unit + 1, (unit + 1) % 2):
                copy.start()

        pl.when(unit % 2 == 0)(functools.partial(arrive, unit // 2))
        up_work(unit, position + 1)
        return carry

    lax.fori_loop(0, units - EARLY, both, 0)
    for copy in final:
        copy.start()
    rank_up[rows:, :] = rank_part[rows:, :].astype(jnp.bfloat16)
    pair_rank(1).start()
    for pair in range(pairs):
        for bit in range(bits):
            swap(bit, 1, pair).wait_send()
    lax.fori_loop(units - EARLY, units, down_unit, 0)
    fold(1, 2).wait_recv()
    for copy in final:
        copy.wait()
    step = 512
    for n in range(span // step):
        cut = slice(n * step, (n + 1) * step)
        acc[:rows, cut] += jnp.dot(rank_down[...], tok[:rows, cut], preferred_element_type=jnp.float32)

    def finish(unit):
        mine, cols = who_rows(0), cols_of(unit, size)
        far = pl.ds(pl.multiple_of(span + unit * size, size), size)
        back(1, unit).wait_recv()
        total = acc[mine, cols] + left[unit // per, :, cols_of(unit % per, size)].astype(jnp.float32)
        for bit in range(bits):
            hand(bit, 0, unit).wait_recv()
            total = total + take[bit, mine, cols].astype(jnp.float32)
        out[:, cols_of(half * units + unit, size)] = total.astype(jnp.bfloat16)
        total = other[:, cols] + jnp.dot(rank_down[...], tok[mine, far], preferred_element_type=jnp.float32)
        back(0, unit).wait_recv()
        total = total + left[quarter + unit // per, :, cols_of(unit % per, size)].astype(jnp.float32)
        out[:, cols_of((1 - half) * units + unit, size)] = total.astype(jnp.bfloat16)
        for stage in range(2):
            for kind in range(7):
                hop(stage, kind, unit).wait_send()
        for bit in range(bits):
            for who in range(2):
                hand(bit, who, unit).wait_send()
        for side in range(2):
            back(side, unit).wait_send()

    def end(unit, carry):
        close(unit)
        finish(unit - units // 2)
        return carry

    lax.fori_loop(units // 2, units, end, 0)
    lax.fori_loop(units // 2, units, lambda unit, carry: (finish(unit), carry)[1], 0)
    for pair in range(pairs):
        for part in range(2):
            lend(part, pair).wait_send()
        for bit in range(bits):
            swap(bit, 0, pair).wait_send()
    for which in range(2):
        pair_rank(which).wait_send()
        for step in range(3):
            fold(which, step).wait_send()


def shards_fused(tokens, up_blocks, up_left, up_right, down_blocks, down_left, down_right):
    rows, features = tokens.shape
    terms, blocks, up_rows, width = up_blocks.shape
    down_rows, size = down_blocks.shape[2:]
    rank = up_left.shape[1]
    count, slabs = lax.axis_size("dp"), lax.axis_size("hid")
    bits = slabs.bit_length() - 1
    units, span = blocks // 2, features // 2
    pairs = units // 2
    any_ = pl.BlockSpec(memory_space=pl.ANY)
    bf, f32 = jnp.bfloat16, jnp.float32
    dma = pltpu.SemaphoreType.DMA
    out, _, _ = pl.pallas_call(
        fused,
        out_shape=(
            jax.ShapeDtypeStruct((rows, features), bf),
            jax.ShapeDtypeStruct((terms, units, count, up_rows, width), bf),
            jax.ShapeDtypeStruct((terms, units, count, down_rows, size), bf),
        ),
        in_specs=[any_] * 7,
        out_specs=(pl.BlockSpec(memory_space=pltpu.VMEM), any_, any_),
        scratch_shapes=[
            pltpu.VMEM((2 * rows, features), bf),
            pltpu.VMEM((bits, 2 * rows, span), bf),
            pltpu.VMEM((bits, 2 * rows, span), bf),
            pltpu.VMEM((features // rows, rows, rank), bf),
            pltpu.VMEM((2 * rows, rank), bf),
            pltpu.VMEM((rows, rank), bf),
            pltpu.VMEM((2 * rows, rank), f32),
            pltpu.VMEM((2, rows, rank), bf),
            pltpu.VMEM((2, 2, rows // 2, rank), bf),
            pltpu.VMEM((rows, rank), bf),
            pltpu.VMEM((2 * rows, units * width), bf),
            pltpu.VMEM((2 * rows, span), f32),
            pltpu.VMEM((rows, span), f32),
            pltpu.VMEM((2, terms, count, up_rows, width), bf),
            pltpu.VMEM((2, rank, width), bf),
            pltpu.VMEM((2, terms, count, down_rows, size), bf),
            pltpu.VMEM((2, width, rank), bf),
            dma((2, 7, units)), dma((2, 7, units)),
            dma((2, pairs)), dma((2, pairs)),
            dma((bits, 2, pairs)), dma((bits, 2, pairs)),
            dma((bits, 2, units)), dma((bits, 2, units)),
            dma((units,)), dma((units,)), dma((units,)), dma((units,)),
            dma((2, 3)), dma((2, 3)),
            dma((2,)), dma((2,)),
            dma((2, count)), dma((2, 2)), dma((2 + features // rows,)),
        ],
        compiler_params=pltpu.CompilerParams(
            collective_id=0, has_side_effects=True, vmem_limit_bytes=62 * 1024 * 1024
        ),
    )(tokens, up_blocks, up_left, up_right, down_blocks, down_left, down_right)
    return out


def shards(tokens, up_blocks, up_left, *rest):
    terms, blocks, up_rows, _ = up_blocks.shape
    rows, features = tokens.shape
    slabs = lax.axis_size("hid")
    reach = blocks.bit_length() - 1 + slabs.bit_length()
    fits = (
        lax.axis_size("dp") == 8
        and up_rows % 16 == 0
        and blocks == 16
        and terms == reach
        and slabs == 4
        and rows == 512
        and features == 4 * rows
        and up_left.shape[1] == rows
    )
    body = shards_fused if fits else shards_plain
    return body(tokens, up_blocks, up_left, *rest)


def solution(mesh):
    placed = (
        P("dp", "hid"),
        P(None, "hid", "dp", None),
        P("hid", None),
        P(None, "hid"),
        P(None, "hid", "dp", None),
        P("hid", None),
        P(None, "hid"),
    )
    return jax.shard_map(
        shards, mesh=mesh, in_specs=placed, out_specs=P("dp", "hid"), check_vma=False
    )
```

```python
import functools

import jax
import jax.numpy as jnp
from jax import lax
from jax.experimental import pallas as pl
from jax.experimental.pallas import tpu as pltpu
from jax.sharding import PartitionSpec as P


def from_partner(block, axis, stride):
    count = lax.axis_size(axis)
    route = []
    for low in range(count):
        high = low | 1 << stride
        if high != low and high < count:
            route += [(low, high), (high, low)]
    return lax.ppermute(block, axis, route)


def swap_blocks(values, block_span, along_axis):
    full_shape = values.shape
    extent = full_shape[along_axis]
    split_shape = (
        full_shape[:along_axis]
        + (extent // (2 * block_span), 2, block_span)
        + full_shape[along_axis + 1 :]
    )
    return jnp.flip(values.reshape(split_shape), along_axis + 1).reshape(full_shape)


def shards_plain(tokens, up_blocks, up_left, up_right, down_blocks, down_left, down_right):
    token_rows = tokens.shape[0]
    local_blocks = up_blocks.shape[1]
    block_size = down_blocks.shape[3]
    term_count = up_blocks.shape[0]
    pieces = tokens.reshape(token_rows, local_blocks, block_size)
    sources = []
    for step_index in range(term_count):
        block_span = 0 if step_index == 0 else 2 ** (step_index - 1)
        if block_span == 0:
            sources.append(pieces)
        elif block_span < local_blocks:
            sources.append(swap_blocks(pieces, block_span, 1))
        else:
            swap_bit = (block_span // local_blocks).bit_length() - 1
            partner_rows = from_partner(tokens, "hid", swap_bit)
            sources.append(partner_rows.reshape(token_rows, local_blocks, block_size))
    stacked = jnp.stack(sources)
    up_full = lax.all_gather(up_blocks, "dp", axis=2, tiled=True)
    hidden_sum = jnp.einsum("tabk,tbkn->abn", stacked, up_full, preferred_element_type=jnp.float32)
    down_full = lax.all_gather(down_blocks, "dp", axis=2, tiled=True)
    rank_up = lax.psum(jnp.dot(tokens, up_left, preferred_element_type=jnp.float32), "hid").astype(
        jnp.bfloat16
    )
    pre_activation = hidden_sum.reshape(
        token_rows, hidden_sum.shape[1] * hidden_sum.shape[2]
    ) + jnp.dot(rank_up, up_right, preferred_element_type=jnp.float32)
    active = jax.nn.gelu(pre_activation, approximate=False).astype(jnp.bfloat16)
    grouped = active.reshape(token_rows, local_blocks, hidden_sum.shape[2])
    contributions = jnp.einsum(
        "abn,tbnk->tabk", grouped, down_full, preferred_element_type=jnp.float32
    )
    out_sum = jnp.zeros((token_rows, local_blocks, block_size), jnp.float32)
    for step_index in range(term_count):
        block_span = 0 if step_index == 0 else 2 ** (step_index - 1)
        if block_span == 0:
            out_sum = contributions[0]
        elif block_span < local_blocks:
            out_sum = out_sum + swap_blocks(contributions[step_index], block_span, 1)
        else:
            swap_bit = (block_span // local_blocks).bit_length() - 1
            out_sum = out_sum + from_partner(contributions[step_index], "hid", swap_bit)
    rank_down = lax.psum(
        jnp.dot(active, down_left, preferred_element_type=jnp.float32), "hid"
    ).astype(jnp.bfloat16)
    result = out_sum.reshape(token_rows, local_blocks * block_size) + jnp.dot(
        rank_down, down_right, preferred_element_type=jnp.float32
    )
    return result.astype(jnp.bfloat16)


EARLY = 4
NEAR = 5
AHEAD = 3
BESIDE = 5
FOLDS = (4, 5, 6)
MESH = pl.DeviceIdType.MESH


def flip(index, bit):
    return index + bit - 2 * bit * ((index // bit) % 2)


def fused(
    tokens, up_blocks, up_left, up_right, down_blocks, down_left, down_right,
    out, up_all, down_all,
    tok, swapped, take, left, rank_up, rank_down, rank_part, rank_send, rank_in, rank_take,
    active, acc, other, w_up, w_right, w_down, w_left,
    sent, got, tok_sent, tok_got, swap_sent, swap_got, give_sent, give_got,
    far_sent, far_got, near_sent, near_got, fold_sent, fold_got,
    pair_sent, pair_got, load_sem, low_sem, pre_sem,
):
    rows = tokens.shape[0]
    terms, blocks = up_blocks.shape[0], up_blocks.shape[1]
    size = down_blocks.shape[3]
    width = up_blocks.shape[3]
    depth = terms * size
    units = blocks // 2
    span = units * size
    me, here = lax.axis_index("dp"), lax.axis_index("hid")
    half = (me // 4) % 2
    slabs = lax.axis_size("hid")
    bits = slabs.bit_length() - 1
    locals_ = terms - bits
    share = rows // 2
    sibling, across, beside = flip(me, 1), flip(me, 2), flip(me, 4)
    diagonal = flip(across, 4)
    pair_cols = 2 * size
    pairs = units // 2
    ranks = (rank_up, rank_down)

    barrier = pltpu.get_barrier_semaphore()
    for near in (sibling, across, beside):
        pl.semaphore_signal(barrier, inc=1, device_id=(near, here), device_id_type=MESH)
    for bit in range(bits):
        pl.semaphore_signal(
            barrier, inc=1, device_id=(me, flip(here, 1 << bit)), device_id_type=MESH
        )
    pl.semaphore_wait(barrier, 3 + bits)

    stages = ((up_blocks, up_all), (down_blocks, down_all))

    def remote(source, target, send, recv, device):
        return pltpu.make_async_remote_copy(
            src_ref=source, dst_ref=target, send_sem=send, recv_sem=recv,
            device_id=device, device_id_type=MESH,
        )

    def cols_of(index, count):
        return pl.ds(pl.multiple_of(index * count, count), count)

    def who_rows(who):
        return pl.ds(who * rows, rows)

    def hop(stage, kind, unit):
        blocks_ref, all_ref = stages[stage]
        if kind < 3:
            side = half if kind < 2 else 1 - half
            source, slot = blocks_ref.at[:, side * units + unit], me
            target = (sibling, across, beside)[kind]
        else:
            slot, target = ((beside, across), (across, sibling), (beside, sibling), (diagonal, sibling))[kind - 3]
        place = all_ref.at[:, unit, slot]
        if kind >= 3:
            source = place
        return remote(source, place, sent.at[stage, kind, unit], got.at[stage, kind, unit], (target, here))

    slots = [me, sibling, across, flip(across, 1), beside, flip(beside, 1), diagonal, flip(diagonal, 1)]
    stored = (w_up, w_down)

    def fetch(stage, unit, count):
        blocks_ref, all_ref = stages[stage]
        return [
            pltpu.make_async_copy(
                blocks_ref.at[:, half * units + unit] if n == 0 else all_ref.at[:, unit, slot],
                stored[stage].at[unit % 2, :, slot], load_sem.at[stage, n],
            )
            for n, slot in enumerate(slots[:count])
        ]

    def send_near(stage, unit):
        hop(stage, 1, unit).start()
        hop(stage, 0, unit).start()

    def send_beside(stage, unit):
        hop(stage, 2, unit).start()

    def forward(stage, unit):
        hop(stage, 2, unit).wait_recv()
        hop(stage, 3, unit).start()
        hop(stage, 5, unit).start()
        hop(stage, 1, unit).wait_recv()
        hop(stage, 4, unit).start()

    def relay(stage, unit):
        hop(stage, 3, unit).wait_recv()
        hop(stage, 6, unit).start()
        for kind in (0, 4, 5):
            hop(stage, kind, unit).wait_recv()
        for copy in fetch(stage, unit, 7):
            copy.start()

    def settle(stage, unit):
        copies = fetch(stage, unit, 8)
        hop(stage, 6, unit).wait_recv()
        copies[-1].start()
        for copy in copies:
            copy.wait()

    late = 2 * units - EARLY

    def act(action, position):
        if isinstance(position, int):
            if position < EARLY:
                action(0, position)
            elif position < late:
                turn = position - EARLY
                action(1 - turn % 2, turn // 2 + EARLY * (turn % 2))
            elif position < 2 * units:
                action(1, position - units)
            return
        turn = position - EARLY
        pl.when(position < EARLY)(lambda: action(0, position))
        between = (position >= EARLY) & (position < late)
        pl.when(between & (turn % 2 == 0))(lambda: action(1, turn // 2))
        pl.when(between & (turn % 2 == 1))(lambda: action(0, turn // 2 + EARLY))
        pl.when((position >= late) & (position < 2 * units))(lambda: action(1, position - units))

    def feed(position):
        act(send_near, position + NEAR)
        act(send_beside, position + BESIDE)

    def pump(position):
        act(relay, position + 1)
        act(forward, position + AHEAD)

    def lend(part, pair):
        side = 1 - half if part == 0 else half
        return remote(
            tokens.at[:, cols_of(side * pairs + pair, pair_cols)],
            tok.at[who_rows(1), pl.ds(pl.multiple_of(part * span + pair * pair_cols, pair_cols), pair_cols)],
            tok_sent.at[part, pair], tok_got.at[part, pair], (beside, here),
        )

    def swap(bit, who, pair):
        cols = cols_of(pair, pair_cols)
        if who == 0:
            source = tokens.at[:, cols_of(half * pairs + pair, pair_cols)]
        else:
            source = tok.at[who_rows(1), cols]
        return remote(
            source, swapped.at[bit, who_rows(who), cols],
            swap_sent.at[bit, who, pair], swap_got.at[bit, who, pair], (me, flip(here, 1 << bit)),
        )

    def swaps(who, pair):
        for bit in reversed(range(bits)):
            swap(bit, who, pair).start()

    def hand(bit, who, unit):
        cols = cols_of(unit, size)
        return remote(
            swapped.at[bit, who_rows(who), cols], take.at[bit, who_rows(who), cols],
            give_sent.at[bit, who, unit], give_got.at[bit, who, unit], (me, flip(here, 1 << bit)),
        )

    quarter = left.shape[0] // 2
    per = units // quarter

    def back(side, unit):
        sends, gets = ((near_sent, near_got), (far_sent, far_got))[side]
        source = pl.ds(pl.multiple_of(side * span + unit * size, size), size)
        return remote(
            tok.at[who_rows(1), source],
            left.at[(1 - side) * quarter + unit // per, :, cols_of(unit % per, size)],
            sends.at[unit], gets.at[unit], (beside, here),
        )

    halves = [
        pl.ds(pl.multiple_of((here % 2) * share, share), share),
        pl.ds(pl.multiple_of((1 - here % 2) * share, share), share),
    ]

    def fold(which, step):
        if step == 0:
            source, target = rank_send.at[which, halves[1]], rank_in.at[which, 0]
        elif step == 1:
            source, target = rank_send.at[which, halves[0]], rank_in.at[which, 1]
        else:
            source = target = ranks[which].at[halves[0]]
        return remote(
            source, target, fold_sent.at[which, step], fold_got.at[which, step],
            (me, flip(here, 2 if step == 1 else 1)),
        )

    def fold_first(which):
        rank_send[which, :, :] = rank_part[:rows, :].astype(jnp.bfloat16)
        fold(which, 0).start()

    def fold_second(which):
        fold(which, 0).wait_recv()
        total = rank_part[halves[0], :] + rank_in[which, 0].astype(jnp.float32)
        rank_part[halves[0], :] = total
        rank_send[which, halves[0], :] = total.astype(jnp.bfloat16)
        fold(which, 1).start()

    def fold_third(which):
        fold(which, 1).wait_recv()
        total = rank_part[halves[0], :] + rank_in[which, 1].astype(jnp.float32)
        ranks[which][halves[0], :] = total.astype(jnp.bfloat16)
        fold(which, 2).start()

    def pair_rank(which):
        if which == 0:
            source, target = rank_up.at[who_rows(0)], rank_up.at[who_rows(1)]
        else:
            source, target = rank_up.at[who_rows(1)], rank_take
        return remote(source, target, pair_sent.at[which], pair_got.at[which], (beside, here))

    chunk = span // quarter

    pre = [
        pltpu.make_async_copy(
            tokens.at[:, cols_of(half * (1 - n) + (1 - half) * n, span)],
            tok.at[who_rows(0), pl.ds(n * span, span)], pre_sem.at[n],
        )
        for n in range(2)
    ]
    for n in range(2):
        for q in range(quarter):
            at = (half * (1 - n) + (1 - half) * n) * quarter + q
            pre.append(pltpu.make_async_copy(
                up_left.at[cols_of(at, chunk)], left.at[n * quarter + q], pre_sem.at[2 + n * quarter + q]
            ))
    final = [
        pltpu.make_async_copy(
            down_right.at[:, cols_of(half * (1 - n) + (1 - half) * n, span)],
            tok.at[who_rows(0), pl.ds(n * span, span)], pre_sem.at[n],
        )
        for n in range(2)
    ]

    def low(unit, slot):
        at = half * units + unit
        return (
            pltpu.make_async_copy(up_right.at[:, cols_of(at, width)], w_right.at[slot], low_sem.at[0, slot]),
            pltpu.make_async_copy(down_left.at[cols_of(at, width)], w_left.at[slot], low_sem.at[1, slot]),
        )

    for copy in pre:
        copy.start()
    lend(0, 0).start()
    lend(0, 1).start()
    act(send_beside, 0)
    act(send_near, 0)
    swap(1, 0, 0).start()
    lend(0, 2).start()
    act(send_beside, 1)
    lend(1, 0).start()
    for position in range(1, NEAR - 1):
        act(send_near, position)
    for copy in low(0, 0):
        copy.start()
    for copy in pre:
        copy.wait()
    total = jnp.dot(tok[:rows, :chunk], left[0], preferred_element_type=jnp.float32)
    for n in range(1, 2 * quarter):
        total += jnp.dot(
            tok[:rows, n * chunk : (n + 1) * chunk], left[n], preferred_element_type=jnp.float32
        )
    rank_part[:rows, :] = total
    fold_first(0)
    swap(0, 0, 0).start()
    acc[...] = jnp.zeros_like(acc)
    fold_second(0)
    swap(1, 0, 1).start()
    lend(0, 0).wait_recv()
    act(forward, 0)
    fold_third(0)
    swaps(1, 0)
    swap(0, 0, 1).start()
    rank_part[...] = jnp.zeros_like(rank_part)
    act(forward, 1)
    act(send_near, NEAR - 1)
    fold(0, 2).wait_recv()
    pair_rank(0).start()
    act(send_beside, 2)
    lend(0, 3).start()
    for position in range(3, BESIDE):
        act(send_beside, position)
    lend(1, 1).start()
    lend(0, 1).wait_recv()
    swaps(1, 1)
    act(relay, 0)
    lend(0, 2).wait_recv()
    swaps(0, 2)
    swaps(1, 2)
    swaps(0, 3)
    for position in range(2, AHEAD):
        act(forward, position)
    pair_rank(0).wait_recv()

    tile = 256

    def up_begin(unit):
        settle(0, unit)

    def up_work(unit, position):
        slot = unit % 2
        for copy in low(unit, slot):
            copy.wait()
        parts = []
        for term in range(terms):
            if term < locals_ - 1:
                at = unit if term == 0 else flip(unit, 1 << (term - 1))
                parts.append(tok[:, cols_of(at, size)])
            elif term == locals_ - 1:
                parts.append(tok[:, pl.ds(pl.multiple_of(span + unit * size, size), size)])
            else:
                parts.append(swapped[term - locals_, :, cols_of(unit, size)])
        source = jnp.concatenate(parts, axis=1)
        coords = rank_up[...]
        for n in range(width // tile):
            cut = slice(n * tile, (n + 1) * tile)
            weights = w_up[slot, :, :, :, cut].reshape(depth, tile)
            pre_act = jnp.dot(source, weights, preferred_element_type=jnp.float32)
            pre_act += jnp.dot(coords, w_right[slot, :, cut], preferred_element_type=jnp.float32)
            value = 0.5 * pre_act * (1.0 + lax.erf(pre_act * (0.5 ** 0.5)))
            start = pl.multiple_of(unit * width + n * tile, tile)
            active[:, pl.ds(start, tile)] = value.astype(jnp.bfloat16)
            if n == width // tile - 2:
                pump(position)
        rank_part[...] += jnp.dot(
            active[:, cols_of(unit, width)], w_left[slot], preferred_element_type=jnp.float32
        )

    def arrive(pair):
        for bit in range(bits):
            for who in range(2):
                swap(bit, who, pair).wait_recv()
        lend(1, pair).wait_recv()

    def up_unit(unit, carry):
        pair = unit // 2
        pl.when((unit % 2 == 1) & (pair + 2 < pairs))(lambda: lend(1, pair + 2).start())
        feed(unit)
        up_begin(unit)

        @pl.when(unit == 2)
        def _():
            lend(0, pairs - 1).wait_recv()
            swaps(1, pairs - 1)

        for copy in low(unit + 1, (unit + 1) % 2):
            copy.start()
        pl.when(unit % 2 == 0)(functools.partial(arrive, pair))
        up_work(unit, unit)
        return carry

    def close(unit):
        mine, cols = who_rows(1), cols_of(unit, size)
        total = acc[mine, cols]
        for bit in range(bits):
            hand(bit, 1, unit).wait_recv()
            total = total + take[bit, mine, cols].astype(jnp.float32)
        tok[mine, cols] = total.astype(jnp.bfloat16)
        back(0, unit).start()

    def down_work(unit, position, middle=lambda: None):
        slot = unit % 2
        source = active[:, cols_of(unit, width)]
        order = [*range(locals_, terms), locals_ - 1, *range(locals_ - 1)]
        for first in range(0, terms, 2):
            pair = order[first : first + 2]
            if first == 4:
                middle()
                pump(position)
            weights = jnp.concatenate([w_down[slot, term].reshape(width, size) for term in pair], axis=1)
            product = jnp.dot(source, weights, preferred_element_type=jnp.float32)
            for n, term in enumerate(pair):
                piece = product[:, n * size : (n + 1) * size]
                if term < locals_ - 1:
                    at = unit if term == 0 else flip(unit, 1 << (term - 1))
                    acc[:, cols_of(at, size)] += piece
                elif term == locals_ - 1:
                    other[:, cols_of(unit, size)] = piece[:rows]
                    far = pl.ds(pl.multiple_of(span + unit * size, size), size)
                    tok[who_rows(1), far] = piece[rows:].astype(jnp.bfloat16)
                    back(1, unit).start()
                else:
                    bit = term - locals_
                    swapped[bit, :, cols_of(unit, size)] = piece.astype(jnp.bfloat16)
                    if term == terms - 1:
                        for who in (1, 0):
                            for bit in reversed(range(bits)):
                                hand(bit, who, unit).start()

    def down_begin(unit):
        settle(1, unit)

    def down_unit(unit, carry):
        feed(unit + units)
        down_begin(unit)

        def middle():
            @pl.when(unit == FOLDS[0])
            def _():
                pair_rank(1).wait_recv()
                rank_part[:rows, :] += rank_take[...].astype(jnp.float32)
                fold_first(1)

            pl.when(unit == FOLDS[1])(lambda: fold_second(1))
            pl.when(unit == FOLDS[2])(lambda: fold_third(1))

        down_work(unit, unit + units, middle)
        pl.when(unit >= units // 2)(lambda: close(unit - units // 2))
        return carry

    lax.fori_loop(0, EARLY, up_unit, 0)

    def both(turn, carry):
        position = EARLY + 2 * turn
        feed(position)
        down_begin(turn)
        down_work(turn, position)
        unit = EARLY + turn
        feed(position + 1)
        up_begin(unit)

        @pl.when(unit + 1 < units)
        def _():
            for copy in low(unit + 1, (unit + 1) % 2):
                copy.start()

        pl.when(unit % 2 == 0)(functools.partial(arrive, unit // 2))
        up_work(unit, position + 1)
        return carry

    lax.fori_loop(0, units - EARLY, both, 0)
    for copy in final:
        copy.start()
    rank_up[rows:, :] = rank_part[rows:, :].astype(jnp.bfloat16)
    pair_rank(1).start()
    for pair in range(pairs):
        for bit in range(bits):
            swap(bit, 1, pair).wait_send()
    lax.fori_loop(units - EARLY, units, down_unit, 0)
    fold(1, 2).wait_recv()
    for copy in final:
        copy.wait()
    step = 512
    for n in range(span // step):
        cut = slice(n * step, (n + 1) * step)
        acc[:rows, cut] += jnp.dot(rank_down[...], tok[:rows, cut], preferred_element_type=jnp.float32)

    def finish(unit):
        mine, cols = who_rows(0), cols_of(unit, size)
        far = pl.ds(pl.multiple_of(span + unit * size, size), size)
        back(1, unit).wait_recv()
        total = acc[mine, cols] + left[unit // per, :, cols_of(unit % per, size)].astype(jnp.float32)
        for bit in range(bits):
            hand(bit, 0, unit).wait_recv()
            total = total + take[bit, mine, cols].astype(jnp.float32)
        out[:, cols_of(half * units + unit, size)] = total.astype(jnp.bfloat16)
        total = other[:, cols] + jnp.dot(rank_down[...], tok[mine, far], preferred_element_type=jnp.float32)
        back(0, unit).wait_recv()
        total = total + left[quarter + unit // per, :, cols_of(unit % per, size)].astype(jnp.float32)
        out[:, cols_of((1 - half) * units + unit, size)] = total.astype(jnp.bfloat16)
        for stage in range(2):
            for kind in range(7):
                hop(stage, kind, unit).wait_send()
        for bit in range(bits):
            for who in range(2):
                hand(bit, who, unit).wait_send()
        for side in range(2):
            back(side, unit).wait_send()

    def end(unit, carry):
        close(unit)
        finish(unit - units // 2)
        return carry

    lax.fori_loop(units // 2, units, end, 0)
    lax.fori_loop(units // 2, units, lambda unit, carry: (finish(unit), carry)[1], 0)
    for pair in range(pairs):
        for part in range(2):
            lend(part, pair).wait_send()
        for bit in range(bits):
            swap(bit, 0, pair).wait_send()
    for which in range(2):
        pair_rank(which).wait_send()
        for step in range(3):
            fold(which, step).wait_send()


def shards_fused(tokens, up_blocks, up_left, up_right, down_blocks, down_left, down_right):
    rows, features = tokens.shape
    terms, blocks, up_rows, width = up_blocks.shape
    down_rows, size = down_blocks.shape[2:]
    rank = up_left.shape[1]
    count, slabs = lax.axis_size("dp"), lax.axis_size("hid")
    bits = slabs.bit_length() - 1
    units, span = blocks // 2, features // 2
    pairs = units // 2
    any_ = pl.BlockSpec(memory_space=pl.ANY)
    bf, f32 = jnp.bfloat16, jnp.float32
    dma = pltpu.SemaphoreType.DMA
    out, _, _ = pl.pallas_call(
        fused,
        out_shape=(
            jax.ShapeDtypeStruct((rows, features), bf),
            jax.ShapeDtypeStruct((terms, units, count, up_rows, width), bf),
            jax.ShapeDtypeStruct((terms, units, count, down_rows, size), bf),
        ),
        in_specs=[any_] * 7,
        out_specs=(pl.BlockSpec(memory_space=pltpu.VMEM), any_, any_),
        scratch_shapes=[
            pltpu.VMEM((2 * rows, features), bf),
            pltpu.VMEM((bits, 2 * rows, span), bf),
            pltpu.VMEM((bits, 2 * rows, span), bf),
            pltpu.VMEM((features // rows, rows, rank), bf),
            pltpu.VMEM((2 * rows, rank), bf),
            pltpu.VMEM((rows, rank), bf),
            pltpu.VMEM((2 * rows, rank), f32),
            pltpu.VMEM((2, rows, rank), bf),
            pltpu.VMEM((2, 2, rows // 2, rank), bf),
            pltpu.VMEM((rows, rank), bf),
            pltpu.VMEM((2 * rows, units * width), bf),
            pltpu.VMEM((2 * rows, span), f32),
            pltpu.VMEM((rows, span), f32),
            pltpu.VMEM((2, terms, count, up_rows, width), bf),
            pltpu.VMEM((2, rank, width), bf),
            pltpu.VMEM((2, terms, count, down_rows, size), bf),
            pltpu.VMEM((2, width, rank), bf),
            dma((2, 7, units)), dma((2, 7, units)),
            dma((2, pairs)), dma((2, pairs)),
            dma((bits, 2, pairs)), dma((bits, 2, pairs)),
            dma((bits, 2, units)), dma((bits, 2, units)),
            dma((units,)), dma((units,)), dma((units,)), dma((units,)),
            dma((2, 3)), dma((2, 3)),
            dma((2,)), dma((2,)),
            dma((2, count)), dma((2, 2)), dma((2 + features // rows,)),
        ],
        compiler_params=pltpu.CompilerParams(
            collective_id=0, has_side_effects=True, vmem_limit_bytes=62 * 1024 * 1024
        ),
    )(tokens, up_blocks, up_left, up_right, down_blocks, down_left, down_right)
    return out


def shards(tokens, up_blocks, up_left, *rest):
    terms, blocks, up_rows, _ = up_blocks.shape
    rows, features = tokens.shape
    slabs = lax.axis_size("hid")
    reach = blocks.bit_length() - 1 + slabs.bit_length()
    fits = (
        lax.axis_size("dp") == 8
        and up_rows % 16 == 0
        and blocks == 16
        and terms == reach
        and slabs == 4
        and rows == 512
        and features == 4 * rows
        and up_left.shape[1] == rows
    )
    body = shards_fused if fits else shards_plain
    return body(tokens, up_blocks, up_left, *rest)


def solution(mesh):
    placed = (
        P("dp", "hid"),
        P(None, "hid", "dp", None),
        P("hid", None),
        P(None, "hid"),
        P(None, "hid", "dp", None),
        P("hid", None),
        P(None, "hid"),
    )
    return jax.shard_map(
        shards, mesh=mesh, in_specs=placed, out_specs=P("dp", "hid"), check_vma=False
    )
```

```python
import functools

import jax
import jax.numpy as jnp
from jax import lax
from jax.experimental import pallas as pl
from jax.experimental.pallas import tpu as pltpu
from jax.sharding import PartitionSpec as P


def from_partner(block, axis, stride):
    count = lax.axis_size(axis)
    route = []
    for low in range(count):
        high = low | 1 << stride
        if high != low and high < count:
            route += [(low, high), (high, low)]
    return lax.ppermute(block, axis, route)


def swap_blocks(values, block_span, along_axis):
    full_shape = values.shape
    extent = full_shape[along_axis]
    split_shape = (
        full_shape[:along_axis]
        + (extent // (2 * block_span), 2, block_span)
        + full_shape[along_axis + 1 :]
    )
    return jnp.flip(values.reshape(split_shape), along_axis + 1).reshape(full_shape)


def shards_plain(tokens, up_blocks, up_left, up_right, down_blocks, down_left, down_right):
    token_rows = tokens.shape[0]
    local_blocks = up_blocks.shape[1]
    block_size = down_blocks.shape[3]
    term_count = up_blocks.shape[0]
    pieces = tokens.reshape(token_rows, local_blocks, block_size)
    sources = []
    for step_index in range(term_count):
        block_span = 0 if step_index == 0 else 2 ** (step_index - 1)
        if block_span == 0:
            sources.append(pieces)
        elif block_span < local_blocks:
            sources.append(swap_blocks(pieces, block_span, 1))
        else:
            swap_bit = (block_span // local_blocks).bit_length() - 1
            partner_rows = from_partner(tokens, "hid", swap_bit)
            sources.append(partner_rows.reshape(token_rows, local_blocks, block_size))
    stacked = jnp.stack(sources)
    up_full = lax.all_gather(up_blocks, "dp", axis=2, tiled=True)
    hidden_sum = jnp.einsum("tabk,tbkn->abn", stacked, up_full, preferred_element_type=jnp.float32)
    down_full = lax.all_gather(down_blocks, "dp", axis=2, tiled=True)
    rank_up = lax.psum(jnp.dot(tokens, up_left, preferred_element_type=jnp.float32), "hid").astype(
        jnp.bfloat16
    )
    pre_activation = hidden_sum.reshape(
        token_rows, hidden_sum.shape[1] * hidden_sum.shape[2]
    ) + jnp.dot(rank_up, up_right, preferred_element_type=jnp.float32)
    active = jax.nn.gelu(pre_activation, approximate=False).astype(jnp.bfloat16)
    grouped = active.reshape(token_rows, local_blocks, hidden_sum.shape[2])
    contributions = jnp.einsum(
        "abn,tbnk->tabk", grouped, down_full, preferred_element_type=jnp.float32
    )
    out_sum = jnp.zeros((token_rows, local_blocks, block_size), jnp.float32)
    for step_index in range(term_count):
        block_span = 0 if step_index == 0 else 2 ** (step_index - 1)
        if block_span == 0:
            out_sum = contributions[0]
        elif block_span < local_blocks:
            out_sum = out_sum + swap_blocks(contributions[step_index], block_span, 1)
        else:
            swap_bit = (block_span // local_blocks).bit_length() - 1
            out_sum = out_sum + from_partner(contributions[step_index], "hid", swap_bit)
    rank_down = lax.psum(
        jnp.dot(active, down_left, preferred_element_type=jnp.float32), "hid"
    ).astype(jnp.bfloat16)
    result = out_sum.reshape(token_rows, local_blocks * block_size) + jnp.dot(
        rank_down, down_right, preferred_element_type=jnp.float32
    )
    return result.astype(jnp.bfloat16)


EARLY = 4
NEAR = 6
AHEAD = 3
BESIDE = 6
FOLDS = (4, 5, 6)
MESH = pl.DeviceIdType.MESH


def flip(index, bit):
    return index + bit - 2 * bit * ((index // bit) % 2)


def fused(
    tokens, up_blocks, up_left, up_right, down_blocks, down_left, down_right,
    out, up_all, down_all,
    tok, swapped, take, left, rank_up, rank_down, rank_part, rank_send, rank_in, rank_take,
    active, acc, other, w_up, w_right, w_down, w_left,
    sent, got, tok_sent, tok_got, swap_sent, swap_got, give_sent, give_got,
    far_sent, far_got, near_sent, near_got, fold_sent, fold_got,
    pair_sent, pair_got, load_sem, low_sem, pre_sem,
):
    rows = tokens.shape[0]
    terms, blocks = up_blocks.shape[0], up_blocks.shape[1]
    size = down_blocks.shape[3]
    width = up_blocks.shape[3]
    depth = terms * size
    units = blocks // 2
    span = units * size
    me, here = lax.axis_index("dp"), lax.axis_index("hid")
    half = (me // 4) % 2
    slabs = lax.axis_size("hid")
    bits = slabs.bit_length() - 1
    locals_ = terms - bits
    share = rows // 2
    sibling, across, beside = flip(me, 1), flip(me, 2), flip(me, 4)
    diagonal = flip(across, 4)
    pair_cols = 2 * size
    pairs = units // 2
    ranks = (rank_up, rank_down)

    barrier = pltpu.get_barrier_semaphore()
    for near in (sibling, across, beside):
        pl.semaphore_signal(barrier, inc=1, device_id=(near, here), device_id_type=MESH)
    for bit in range(bits):
        pl.semaphore_signal(
            barrier, inc=1, device_id=(me, flip(here, 1 << bit)), device_id_type=MESH
        )
    pl.semaphore_wait(barrier, 3 + bits)

    stages = ((up_blocks, up_all), (down_blocks, down_all))

    def remote(source, target, send, recv, device):
        return pltpu.make_async_remote_copy(
            src_ref=source, dst_ref=target, send_sem=send, recv_sem=recv,
            device_id=device, device_id_type=MESH,
        )

    def cols_of(index, count):
        return pl.ds(pl.multiple_of(index * count, count), count)

    def who_rows(who):
        return pl.ds(who * rows, rows)

    def hop(stage, kind, unit):
        blocks_ref, all_ref = stages[stage]
        if kind < 3:
            side = half if kind < 2 else 1 - half
            source, slot = blocks_ref.at[:, side * units + unit], me
            target = (sibling, across, beside)[kind]
        else:
            slot, target = ((beside, across), (across, sibling), (beside, sibling), (diagonal, sibling))[kind - 3]
        place = all_ref.at[:, unit, slot]
        if kind >= 3:
            source = place
        return remote(source, place, sent.at[stage, kind, unit], got.at[stage, kind, unit], (target, here))

    slots = [me, sibling, across, flip(across, 1), beside, flip(beside, 1), diagonal, flip(diagonal, 1)]
    stored = (w_up, w_down)

    def fetch(stage, unit, count):
        blocks_ref, all_ref = stages[stage]
        return [
            pltpu.make_async_copy(
                blocks_ref.at[:, half * units + unit] if n == 0 else all_ref.at[:, unit, slot],
                stored[stage].at[unit % 2, :, slot], load_sem.at[stage, n],
            )
            for n, slot in enumerate(slots[:count])
        ]

    def send_near(stage, unit):
        hop(stage, 1, unit).start()
        hop(stage, 0, unit).start()

    def send_beside(stage, unit):
        hop(stage, 2, unit).start()

    def forward(stage, unit):
        hop(stage, 2, unit).wait_recv()
        hop(stage, 3, unit).start()
        hop(stage, 5, unit).start()
        hop(stage, 1, unit).wait_recv()
        hop(stage, 4, unit).start()

    def relay(stage, unit):
        hop(stage, 3, unit).wait_recv()
        hop(stage, 6, unit).start()
        for kind in (0, 4, 5):
            hop(stage, kind, unit).wait_recv()
        for copy in fetch(stage, unit, 7):
            copy.start()

    def settle(stage, unit):
        copies = fetch(stage, unit, 8)
        hop(stage, 6, unit).wait_recv()
        copies[-1].start()
        for copy in copies:
            copy.wait()

    late = 2 * units - EARLY

    def act(action, position):
        if isinstance(position, int):
            if position < EARLY:
                action(0, position)
            elif position < late:
                turn = position - EARLY
                action(1 - turn % 2, turn // 2 + EARLY * (turn % 2))
            elif position < 2 * units:
                action(1, position - units)
            return
        turn = position - EARLY
        pl.when(position < EARLY)(lambda: action(0, position))
        between = (position >= EARLY) & (position < late)
        pl.when(between & (turn % 2 == 0))(lambda: action(1, turn // 2))
        pl.when(between & (turn % 2 == 1))(lambda: action(0, turn // 2 + EARLY))
        pl.when((position >= late) & (position < 2 * units))(lambda: action(1, position - units))

    def feed(position):
        act(send_near, position + NEAR)
        act(send_beside, position + BESIDE)

    def pump(position):
        act(relay, position + 1)
        act(forward, position + AHEAD)

    def lend(part, pair):
        side = 1 - half if part == 0 else half
        return remote(
            tokens.at[:, cols_of(side * pairs + pair, pair_cols)],
            tok.at[who_rows(1), pl.ds(pl.multiple_of(part * span + pair * pair_cols, pair_cols), pair_cols)],
            tok_sent.at[part, pair], tok_got.at[part, pair], (beside, here),
        )

    def swap(bit, who, pair):
        cols = cols_of(pair, pair_cols)
        if who == 0:
            source = tokens.at[:, cols_of(half * pairs + pair, pair_cols)]
        else:
            source = tok.at[who_rows(1), cols]
        return remote(
            source, swapped.at[bit, who_rows(who), cols],
            swap_sent.at[bit, who, pair], swap_got.at[bit, who, pair], (me, flip(here, 1 << bit)),
        )

    def swaps(who, pair):
        for bit in reversed(range(bits)):
            swap(bit, who, pair).start()

    def hand(bit, who, unit):
        cols = cols_of(unit, size)
        return remote(
            swapped.at[bit, who_rows(who), cols], take.at[bit, who_rows(who), cols],
            give_sent.at[bit, who, unit], give_got.at[bit, who, unit], (me, flip(here, 1 << bit)),
        )

    quarter = left.shape[0] // 2
    per = units // quarter

    def back(side, unit):
        sends, gets = ((near_sent, near_got), (far_sent, far_got))[side]
        source = pl.ds(pl.multiple_of(side * span + unit * size, size), size)
        return remote(
            tok.at[who_rows(1), source],
            left.at[(1 - side) * quarter + unit // per, :, cols_of(unit % per, size)],
            sends.at[unit], gets.at[unit], (beside, here),
        )

    halves = [
        pl.ds(pl.multiple_of((here % 2) * share, share), share),
        pl.ds(pl.multiple_of((1 - here % 2) * share, share), share),
    ]

    def fold(which, step):
        if step == 0:
            source, target = rank_send.at[which, halves[1]], rank_in.at[which, 0]
        elif step == 1:
            source, target = rank_send.at[which, halves[0]], rank_in.at[which, 1]
        else:
            source = target = ranks[which].at[halves[0]]
        return remote(
            source, target, fold_sent.at[which, step], fold_got.at[which, step],
            (me, flip(here, 2 if step == 1 else 1)),
        )

    def fold_first(which):
        rank_send[which, :, :] = rank_part[:rows, :].astype(jnp.bfloat16)
        fold(which, 0).start()

    def fold_second(which):
        fold(which, 0).wait_recv()
        total = rank_part[halves[0], :] + rank_in[which, 0].astype(jnp.float32)
        rank_part[halves[0], :] = total
        rank_send[which, halves[0], :] = total.astype(jnp.bfloat16)
        fold(which, 1).start()

    def fold_third(which):
        fold(which, 1).wait_recv()
        total = rank_part[halves[0], :] + rank_in[which, 1].astype(jnp.float32)
        ranks[which][halves[0], :] = total.astype(jnp.bfloat16)
        fold(which, 2).start()

    def pair_rank(which):
        if which == 0:
            source, target = rank_up.at[who_rows(0)], rank_up.at[who_rows(1)]
        else:
            source, target = rank_up.at[who_rows(1)], rank_take
        return remote(source, target, pair_sent.at[which], pair_got.at[which], (beside, here))

    chunk = span // quarter

    pre = [
        pltpu.make_async_copy(
            tokens.at[:, cols_of(half * (1 - n) + (1 - half) * n, span)],
            tok.at[who_rows(0), pl.ds(n * span, span)], pre_sem.at[n],
        )
        for n in range(2)
    ]
    for n in range(2):
        for q in range(quarter):
            at = (half * (1 - n) + (1 - half) * n) * quarter + q
            pre.append(pltpu.make_async_copy(
                up_left.at[cols_of(at, chunk)], left.at[n * quarter + q], pre_sem.at[2 + n * quarter + q]
            ))
    final = [
        pltpu.make_async_copy(
            down_right.at[:, cols_of(half * (1 - n) + (1 - half) * n, span)],
            tok.at[who_rows(0), pl.ds(n * span, span)], pre_sem.at[n],
        )
        for n in range(2)
    ]

    def low(unit, slot):
        at = half * units + unit
        return (
            pltpu.make_async_copy(up_right.at[:, cols_of(at, width)], w_right.at[slot], low_sem.at[0, slot]),
            pltpu.make_async_copy(down_left.at[cols_of(at, width)], w_left.at[slot], low_sem.at[1, slot]),
        )

    for copy in pre:
        copy.start()
    lend(0, 0).start()
    lend(0, 1).start()
    act(send_beside, 0)
    act(send_near, 0)
    swap(1, 0, 0).start()
    lend(0, 2).start()
    act(send_beside, 1)
    lend(1, 0).start()
    for position in range(1, NEAR - 1):
        act(send_near, position)
    for copy in low(0, 0):
        copy.start()
    for copy in pre:
        copy.wait()
    total = jnp.dot(tok[:rows, :chunk], left[0], preferred_element_type=jnp.float32)
    for n in range(1, 2 * quarter):
        total += jnp.dot(
            tok[:rows, n * chunk : (n + 1) * chunk], left[n], preferred_element_type=jnp.float32
        )
    rank_part[:rows, :] = total
    fold_first(0)
    swap(0, 0, 0).start()
    acc[...] = jnp.zeros_like(acc)
    fold_second(0)
    swap(1, 0, 1).start()
    lend(0, 0).wait_recv()
    act(forward, 0)
    fold_third(0)
    swaps(1, 0)
    swap(0, 0, 1).start()
    rank_part[...] = jnp.zeros_like(rank_part)
    act(forward, 1)
    act(send_near, NEAR - 1)
    fold(0, 2).wait_recv()
    pair_rank(0).start()
    act(send_beside, 2)
    lend(0, 3).start()
    for position in range(3, BESIDE):
        act(send_beside, position)
    lend(1, 1).start()
    lend(0, 1).wait_recv()
    swaps(1, 1)
    act(relay, 0)
    lend(0, 2).wait_recv()
    swaps(0, 2)
    swaps(1, 2)
    swaps(0, 3)
    for position in range(2, AHEAD):
        act(forward, position)
    pair_rank(0).wait_recv()

    tile = 256

    def up_begin(unit):
        settle(0, unit)

    def up_work(unit, position):
        slot = unit % 2
        for copy in low(unit, slot):
            copy.wait()
        parts = []
        for term in range(terms):
            if term < locals_ - 1:
                at = unit if term == 0 else flip(unit, 1 << (term - 1))
                parts.append(tok[:, cols_of(at, size)])
            elif term == locals_ - 1:
                parts.append(tok[:, pl.ds(pl.multiple_of(span + unit * size, size), size)])
            else:
                parts.append(swapped[term - locals_, :, cols_of(unit, size)])
        source = jnp.concatenate(parts, axis=1)
        coords = rank_up[...]
        for n in range(width // tile):
            cut = slice(n * tile, (n + 1) * tile)
            weights = w_up[slot, :, :, :, cut].reshape(depth, tile)
            pre_act = jnp.dot(source, weights, preferred_element_type=jnp.float32)
            pre_act += jnp.dot(coords, w_right[slot, :, cut], preferred_element_type=jnp.float32)
            value = 0.5 * pre_act * (1.0 + lax.erf(pre_act * (0.5 ** 0.5)))
            start = pl.multiple_of(unit * width + n * tile, tile)
            active[:, pl.ds(start, tile)] = value.astype(jnp.bfloat16)
            if n == width // tile - 2:
                pump(position)
        rank_part[...] += jnp.dot(
            active[:, cols_of(unit, width)], w_left[slot], preferred_element_type=jnp.float32
        )

    def arrive(pair):
        for bit in range(bits):
            for who in range(2):
                swap(bit, who, pair).wait_recv()
        lend(1, pair).wait_recv()

    def up_unit(unit, carry):
        pair = unit // 2
        pl.when((unit % 2 == 1) & (pair + 2 < pairs))(lambda: lend(1, pair + 2).start())
        feed(unit)
        up_begin(unit)

        @pl.when(unit == 2)
        def _():
            lend(0, pairs - 1).wait_recv()
            swaps(1, pairs - 1)

        for copy in low(unit + 1, (unit + 1) % 2):
            copy.start()
        pl.when(unit % 2 == 0)(functools.partial(arrive, pair))
        up_work(unit, unit)
        return carry

    def close(unit):
        mine, cols = who_rows(1), cols_of(unit, size)
        total = acc[mine, cols]
        for bit in range(bits):
            hand(bit, 1, unit).wait_recv()
            total = total + take[bit, mine, cols].astype(jnp.float32)
        tok[mine, cols] = total.astype(jnp.bfloat16)
        back(0, unit).start()

    def down_work(unit, position, middle=lambda: None):
        slot = unit % 2
        source = active[:, cols_of(unit, width)]
        order = [*range(locals_, terms), locals_ - 1, *range(locals_ - 1)]
        for first in range(0, terms, 2):
            pair = order[first : first + 2]
            if first == 4:
                middle()
                pump(position)
            weights = jnp.concatenate([w_down[slot, term].reshape(width, size) for term in pair], axis=1)
            product = jnp.dot(source, weights, preferred_element_type=jnp.float32)
            for n, term in enumerate(pair):
                piece = product[:, n * size : (n + 1) * size]
                if term < locals_ - 1:
                    at = unit if term == 0 else flip(unit, 1 << (term - 1))
                    acc[:, cols_of(at, size)] += piece
                elif term == locals_ - 1:
                    other[:, cols_of(unit, size)] = piece[:rows]
                    far = pl.ds(pl.multiple_of(span + unit * size, size), size)
                    tok[who_rows(1), far] = piece[rows:].astype(jnp.bfloat16)
                    back(1, unit).start()
                else:
                    bit = term - locals_
                    swapped[bit, :, cols_of(unit, size)] = piece.astype(jnp.bfloat16)
                    if term == terms - 1:
                        for who in (1, 0):
                            for bit in reversed(range(bits)):
                                hand(bit, who, unit).start()

    def down_begin(unit):
        settle(1, unit)

    def down_unit(unit, carry):
        feed(unit + units)
        down_begin(unit)

        def middle():
            @pl.when(unit == FOLDS[0])
            def _():
                pair_rank(1).wait_recv()
                rank_part[:rows, :] += rank_take[...].astype(jnp.float32)
                fold_first(1)

            pl.when(unit == FOLDS[1])(lambda: fold_second(1))
            pl.when(unit == FOLDS[2])(lambda: fold_third(1))

        down_work(unit, unit + units, middle)
        pl.when(unit >= units // 2)(lambda: close(unit - units // 2))
        return carry

    lax.fori_loop(0, EARLY, up_unit, 0)

    def both(turn, carry):
        position = EARLY + 2 * turn
        feed(position)
        down_begin(turn)
        down_work(turn, position)
        unit = EARLY + turn
        feed(position + 1)
        up_begin(unit)

        @pl.when(unit + 1 < units)
        def _():
            for copy in low(unit + 1, (unit + 1) % 2):
                copy.start()

        pl.when(unit % 2 == 0)(functools.partial(arrive, unit // 2))
        up_work(unit, position + 1)
        return carry

    lax.fori_loop(0, units - EARLY, both, 0)
    for copy in final:
        copy.start()
    rank_up[rows:, :] = rank_part[rows:, :].astype(jnp.bfloat16)
    pair_rank(1).start()
    for pair in range(pairs):
        for bit in range(bits):
            swap(bit, 1, pair).wait_send()
    lax.fori_loop(units - EARLY, units, down_unit, 0)
    fold(1, 2).wait_recv()
    for copy in final:
        copy.wait()
    step = 512
    for n in range(span // step):
        cut = slice(n * step, (n + 1) * step)
        acc[:rows, cut] += jnp.dot(rank_down[...], tok[:rows, cut], preferred_element_type=jnp.float32)

    def finish(unit):
        mine, cols = who_rows(0), cols_of(unit, size)
        far = pl.ds(pl.multiple_of(span + unit * size, size), size)
        back(1, unit).wait_recv()
        total = acc[mine, cols] + left[unit // per, :, cols_of(unit % per, size)].astype(jnp.float32)
        for bit in range(bits):
            hand(bit, 0, unit).wait_recv()
            total = total + take[bit, mine, cols].astype(jnp.float32)
        out[:, cols_of(half * units + unit, size)] = total.astype(jnp.bfloat16)
        total = other[:, cols] + jnp.dot(rank_down[...], tok[mine, far], preferred_element_type=jnp.float32)
        back(0, unit).wait_recv()
        total = total + left[quarter + unit // per, :, cols_of(unit % per, size)].astype(jnp.float32)
        out[:, cols_of((1 - half) * units + unit, size)] = total.astype(jnp.bfloat16)
        for stage in range(2):
            for kind in range(7):
                hop(stage, kind, unit).wait_send()
        for bit in range(bits):
            for who in range(2):
                hand(bit, who, unit).wait_send()
        for side in range(2):
            back(side, unit).wait_send()

    def end(unit, carry):
        close(unit)
        finish(unit - units // 2)
        return carry

    lax.fori_loop(units // 2, units, end, 0)
    lax.fori_loop(units // 2, units, lambda unit, carry: (finish(unit), carry)[1], 0)
    for pair in range(pairs):
        for part in range(2):
            lend(part, pair).wait_send()
        for bit in range(bits):
            swap(bit, 0, pair).wait_send()
    for which in range(2):
        pair_rank(which).wait_send()
        for step in range(3):
            fold(which, step).wait_send()


def shards_fused(tokens, up_blocks, up_left, up_right, down_blocks, down_left, down_right):
    rows, features = tokens.shape
    terms, blocks, up_rows, width = up_blocks.shape
    down_rows, size = down_blocks.shape[2:]
    rank = up_left.shape[1]
    count, slabs = lax.axis_size("dp"), lax.axis_size("hid")
    bits = slabs.bit_length() - 1
    units, span = blocks // 2, features // 2
    pairs = units // 2
    any_ = pl.BlockSpec(memory_space=pl.ANY)
    bf, f32 = jnp.bfloat16, jnp.float32
    dma = pltpu.SemaphoreType.DMA
    out, _, _ = pl.pallas_call(
        fused,
        out_shape=(
            jax.ShapeDtypeStruct((rows, features), bf),
            jax.ShapeDtypeStruct((terms, units, count, up_rows, width), bf),
            jax.ShapeDtypeStruct((terms, units, count, down_rows, size), bf),
        ),
        in_specs=[any_] * 7,
        out_specs=(pl.BlockSpec(memory_space=pltpu.VMEM), any_, any_),
        scratch_shapes=[
            pltpu.VMEM((2 * rows, features), bf),
            pltpu.VMEM((bits, 2 * rows, span), bf),
            pltpu.VMEM((bits, 2 * rows, span), bf),
            pltpu.VMEM((features // rows, rows, rank), bf),
            pltpu.VMEM((2 * rows, rank), bf),
            pltpu.VMEM((rows, rank), bf),
            pltpu.VMEM((2 * rows, rank), f32),
            pltpu.VMEM((2, rows, rank), bf),
            pltpu.VMEM((2, 2, rows // 2, rank), bf),
            pltpu.VMEM((rows, rank), bf),
            pltpu.VMEM((2 * rows, units * width), bf),
            pltpu.VMEM((2 * rows, span), f32),
            pltpu.VMEM((rows, span), f32),
            pltpu.VMEM((2, terms, count, up_rows, width), bf),
            pltpu.VMEM((2, rank, width), bf),
            pltpu.VMEM((2, terms, count, down_rows, size), bf),
            pltpu.VMEM((2, width, rank), bf),
            dma((2, 7, units)), dma((2, 7, units)),
            dma((2, pairs)), dma((2, pairs)),
            dma((bits, 2, pairs)), dma((bits, 2, pairs)),
            dma((bits, 2, units)), dma((bits, 2, units)),
            dma((units,)), dma((units,)), dma((units,)), dma((units,)),
            dma((2, 3)), dma((2, 3)),
            dma((2,)), dma((2,)),
            dma((2, count)), dma((2, 2)), dma((2 + features // rows,)),
        ],
        compiler_params=pltpu.CompilerParams(
            collective_id=0, has_side_effects=True, vmem_limit_bytes=62 * 1024 * 1024
        ),
    )(tokens, up_blocks, up_left, up_right, down_blocks, down_left, down_right)
    return out


def shards(tokens, up_blocks, up_left, *rest):
    terms, blocks, up_rows, _ = up_blocks.shape
    rows, features = tokens.shape
    slabs = lax.axis_size("hid")
    reach = blocks.bit_length() - 1 + slabs.bit_length()
    fits = (
        lax.axis_size("dp") == 8
        and up_rows % 16 == 0
        and blocks == 16
        and terms == reach
        and slabs == 4
        and rows == 512
        and features == 4 * rows
        and up_left.shape[1] == rows
    )
    body = shards_fused if fits else shards_plain
    return body(tokens, up_blocks, up_left, *rest)


def solution(mesh):
    placed = (
        P("dp", "hid"),
        P(None, "hid", "dp", None),
        P("hid", None),
        P(None, "hid"),
        P(None, "hid", "dp", None),
        P("hid", None),
        P(None, "hid"),
    )
    return jax.shard_map(
        shards, mesh=mesh, in_specs=placed, out_specs=P("dp", "hid"), check_vma=False
    )
```
